32 devices in a mesh: groups: 2 (over x), dev: 16 (over z, y, core).
Axes of the slice: x: 2, y: 2, z: 4, core: 2. Of those that a mesh axis runs over, the one named last changes fastest.
Arguments:
- hidden_in: bfloat16 [512, 4096], P(('groups', 'dev')), parts along dimension 0, may hold values from -2 to 2
- queries: bfloat16 [512, 4096], P(('groups', 'dev')), parts along dimension 0, may hold values from -80 to 80
- fresh_key_value: bfloat16 [512, 2, 256], P(('groups', 'dev')), parts along dimension 0, may hold values from -6 to 6
- segment_key_cache: bfloat16 [4096, 16, 256], P(('groups', 'dev')), parts along dimension 0, may hold values from -6 to 6
- segment_value_cache: bfloat16 [4096, 16, 256], P(('groups', 'dev')), parts along dimension 0, may hold values from -6 to 6
- segment_owner_row: int32 [4096], P(('groups', 'dev')), parts along dimension 0, may hold values from 0 to 255, as said below
- segment_length: int32 [4096], P(('groups', 'dev')), parts along dimension 0, may hold values from 1 to 16
- expert_ids: int32 [512, 8], P(('groups', 'dev')), parts along dimension 0, may hold values from 0 to 15, all different within a row; in each aligned block of 16 rows (0 to 15, 16 to 31, ...) at most 8 rows name the same one
- gate_score: int32 [512, 8], P(('groups', 'dev')), parts along dimension 0, may hold values from 0 to 11
- out_proj: bfloat16 [4096, 4096], P('dev'), may hold values from -0.09375 to 0.09375
- norm_gain: bfloat16 [4096], replicated, may hold values from 0.099609375 to 1.8984375
- w_gate: bfloat16 [16, 4096, 768], P('dev'), may hold values from -0.09375 to 0.09375
- w_up: bfloat16 [16, 4096, 768], P('dev'), may hold values from -0.09375 to 0.09375
- w_down: bfloat16 [16, 768, 4096], P('dev'), may hold values from -0.21875 to 0.21875
Outputs:
- layer_out: bfloat16 [512, 4096], P(('groups', 'dev')), parts along dimension 0
The draws below stay inside these ranges and needn't reach their ends.
There are 2 independent parts, one for each index of `groups`. The reference program is written for one: setup_inputs(seed, part) draws one part's arguments, and reference() takes and returns one part's arrays. A program takes and returns all parts, laid end to end along the dimension named above; an argument that names none is the same for every part. Nothing has to cross between parts.
Inputs may be any that keep to these rules, and one draw needn't show every extreme that they name: `segment_owner_row`: segment rows never fall along the segments, and every row owns at least one segment. `expert_ids`: each row names 8 different experts; among the rows of one device no expert is named by more than 8 rows.
All inputs are finite; a program needn't handle non-finite values.
Results may differ from the reference program's by a relative error of at most 0.024.
Values may be sent and summed in bfloat16 or wider, within the bound.
No kernel may reach another device: no remote copies, remote signals or barrier semaphores. Data moves between devices by JAX's collectives and lax.ppermute only.
A program may use at most 128 MiB of HBM per device.

```python
import math
import jax
import jax.numpy as jnp
import numpy as np
from jax import lax

D = 4096
HEAD_SIZE = 128
TOP = 8
HQ = 32
KEY_VALUE_HEADS = 2
FF = 768
SEGMENT_SLOTS = 16
ROW_DEV = 16
DEVICE_SEGMENTS = 128
DECODE_ROWS = 256
CACHE_SEGMENTS = 2048
EXPERTS = 16
CAP = 8
HPD = 2
N_DEV = 16


def draw_queries(key, part):
    base_values = jnp.clip(jax.random.normal(key, (DECODE_ROWS, HQ * HEAD_SIZE), jnp.float32), -5.0, 5.0)
    return base_values.astype(jnp.bfloat16)


def split_runs(key, length, count):
    cut_points = jnp.sort(jax.random.permutation(key, length - 1)[:count - 1].astype(jnp.int32) + 1)
    positions = jnp.arange(length, dtype=jnp.int32)
    return jnp.sum((positions[:, None] >= cut_points[None, :]).astype(jnp.int32), axis=1).astype(jnp.int32)


def draw_segment_owner_row(key, part):
    half_devices = N_DEV // 2
    head_length = half_devices * DEVICE_SEGMENTS + 1
    middle_length = DEVICE_SEGMENTS - 1
    tail_length = CACHE_SEGMENTS - (half_devices + 1) * DEVICE_SEGMENTS
    head_rows = jnp.zeros((head_length,), jnp.int32)
    middle_rows = 1 + split_runs(jax.random.fold_in(key, 11), middle_length, ROW_DEV - 1)
    tail_rows = ROW_DEV + split_runs(jax.random.fold_in(key, 13), tail_length, DECODE_ROWS - ROW_DEV)
    return jnp.concatenate([head_rows, middle_rows.astype(jnp.int32), tail_rows.astype(jnp.int32)]).astype(jnp.int32)


def set_ends(entries, rng, low, top_value):
    extent = entries.shape
    spot = [jax.random.randint(jax.random.fold_in(rng, axis), (), 0, extent[axis]) for axis in range(len(extent))]
    entries = entries.at[tuple(spot)].set(low)
    longest = extent.index(max(extent))
    spot[longest] = (spot[longest] + 1) % extent[longest]
    return entries.at[tuple(spot)].set(top_value)


def level_of(key, dims, cuts, least, largest):
    def one(dim, shards_of):
        draws = jax.random.uniform(jax.random.fold_in(jax.random.fold_in(key, 6), dim), (shards_of,), jnp.float32, least / len(cuts), largest / len(cuts))
        return jnp.repeat(jnp.exp(draws), dims[dim] // shards_of).reshape((-1,) + (1,) * (len(dims) - dim - 1))

    gain = one(*cuts[0])
    for cut in cuts[1:]:
        gain = gain * one(*cut)
    return gain


def assign_block(stream_key, own, number, rows, amount, top, reach, lean):
    order = jax.random.permutation(stream_key, amount)
    heavy_load, usual = portions_of(amount, rows * top, reach, lean, True), portions_of(amount, rows * top, reach, lean, False)
    places = jnp.arange(amount)

    def named(tallies, turn):
        used = int((tallies > 0).sum())
        fixed = max(1, used // 4)
        shifted = fixed + (places - fixed + turn * (used - fixed)) % max(1, amount - fixed)
        return jnp.zeros((amount,), jnp.int32).at[order[jnp.where(places < fixed, places, shifted)]].set(jnp.asarray(tallies, jnp.int32))

    tallies = jnp.where(number % 4 == 0, named(heavy_load, number // 4), named(usual, number - number // 4 - 1))
    mixed = jax.random.permutation(jax.random.fold_in(own, 3), amount)
    donor, sink = mixed[0:amount // 2 * 2:2], mixed[1:amount // 2 * 2:2]
    room = jnp.minimum(tallies[donor] - 1, reach - tallies[sink]) // 2
    room = jnp.where((donor == order[0]) | (sink == order[0]) | (tallies[sink] == 0), 0, jnp.maximum(room, 0))
    shifted = jax.random.randint(jax.random.fold_in(own, 4), (amount // 2,), 0, 1 << 20) % (room + 1)
    tallies = tallies.at[donor].add(-shifted).at[sink].add(shifted)
    items = jnp.searchsorted(jnp.cumsum(tallies), jnp.arange(rows * top), side="right").astype(jnp.int32)
    listing = items.reshape(top, rows).T
    listing = listing[jax.random.permutation(jax.random.fold_in(own, 1), rows)]
    turn = jax.random.randint(jax.random.fold_in(own, 2), (rows, 1), 0, top)
    return jnp.take_along_axis(listing, (jnp.arange(top)[None, :] + turn) % top, axis=1)


def portions_of(count, total, most, skew, full):
    weights = [(1 << 20) // math.isqrt(grade ** skew) + 1 for grade in range(1, count + 1)]
    largest = most if full else min(most, max(-(-total // count), total * weights[0] // sum(weights)))
    least = 1 if total - largest >= count - 1 else 0
    given, surplus = [largest] + [least] * (count - 1), total - largest - least * (count - 1)
    while surplus > 0:
        movable = [i for i in range(1, count) if given[i] < largest] or [i for i in range(1, count) if given[i] < most]
        mass, left = sum([weights[i] for i in movable]), surplus
        for i in movable:
            extra = min(most - given[i], max(1, left * weights[i] // mass), surplus)
            given[i] = given[i] + extra
            surplus = surplus - extra
    return np.array(given)


def noise(key, shape, spread, reach, shards=(), kind=jnp.bfloat16):
    values = jax.random.normal(key, shape, jnp.float32) * spread
    if len(shards) > 0:
        values = level_of(key, shape, shards, -0.22, 0.18) * values
    return jnp.clip(values, min=-reach, max=reach).astype(kind)


def setup_inputs(seed: int = 0, part: int = 0) -> dict:
    key_list = jax.random.split(jax.random.key(seed), 15)
    part_splits = jax.random.split(jax.random.fold_in(key_list[14], part), 15)
    hidden_in = noise(part_splits[0], (DECODE_ROWS, D), 0.3, 2.0, ((0, 16),))
    queries = draw_queries(jax.random.fold_in(jax.random.fold_in(key_list[14], part), 71), part)
    fresh_key_value = noise(part_splits[2], (DECODE_ROWS, 2, KEY_VALUE_HEADS * HEAD_SIZE), 1.0, 6.0, ((0, 16),))
    segment_key_cache = noise(part_splits[3], (CACHE_SEGMENTS, SEGMENT_SLOTS, KEY_VALUE_HEADS * HEAD_SIZE), 1.0, 6.0, ((0, 16),))
    segment_value_cache = noise(part_splits[4], (CACHE_SEGMENTS, SEGMENT_SLOTS, KEY_VALUE_HEADS * HEAD_SIZE), 1.0, 6.0, ((0, 16),))
    segment_owner_row = draw_segment_owner_row(jax.random.fold_in(jax.random.fold_in(key_list[14], part), 71), part)
    segment_length = set_ends(jax.random.randint(part_splits[6], (CACHE_SEGMENTS,), 1, SEGMENT_SLOTS + 1), jax.random.fold_in(part_splits[6], 1), 1, SEGMENT_SLOTS).astype(jnp.int32)
    expert_ids_keys = jax.random.split(jax.random.fold_in(part_splits[7], 1), DECODE_ROWS // ROW_DEV)
    expert_ids_turns = jax.random.permutation(jax.random.fold_in(part_splits[7], 3), DECODE_ROWS // ROW_DEV)
    expert_ids = jax.vmap(lambda own, number: assign_block(jax.random.fold_in(part_splits[7], 2), own, number, ROW_DEV, EXPERTS, TOP, CAP, 2))(expert_ids_keys, expert_ids_turns).reshape((DECODE_ROWS, TOP))
    gate_score = set_ends(jax.random.randint(part_splits[8], (DECODE_ROWS, TOP), 0, 12), jax.random.fold_in(part_splits[8], 1), 0, 11).astype(jnp.int32)
    out_proj = noise(key_list[9], (HQ * HEAD_SIZE, D), (HQ * HEAD_SIZE) ** -0.5, 0.09375, ((0, 16),))
    norm_gain = jnp.clip(1.0 + 0.18 * jax.random.normal(key_list[10], (D,), jnp.float32), 0.099609375, 1.8984375).astype(jnp.bfloat16)
    w_gate = noise(key_list[11], (EXPERTS, D, FF), D ** -0.5, 0.09375, ((0, 16),))
    w_up = noise(key_list[12], (EXPERTS, D, FF), D ** -0.5, 0.09375, ((0, 16),))
    w_down = noise(key_list[13], (EXPERTS, FF, D), FF ** -0.5, 0.21875, ((0, 16),))
    return dict(hidden_in=hidden_in, queries=queries, fresh_key_value=fresh_key_value, segment_key_cache=segment_key_cache, segment_value_cache=segment_value_cache, segment_owner_row=segment_owner_row, segment_length=segment_length, expert_ids=expert_ids, gate_score=gate_score, out_proj=out_proj, norm_gain=norm_gain, w_gate=w_gate, w_up=w_up, w_down=w_down)


FLOOR_MAX = -1e+30

def segment_terms(query_rows, key_cache, value_cache, seg_lengths):
    seg_count = key_cache.shape[0]
    seg_width = key_cache.shape[1]
    kv_heads = key_cache.shape[2] // HEAD_SIZE
    group_size = HQ // kv_heads
    query_blocks = query_rows.reshape(seg_count, kv_heads, group_size, HEAD_SIZE).astype(jnp.float32)
    key_blocks = key_cache.reshape(seg_count, seg_width, kv_heads, HEAD_SIZE).astype(jnp.float32)
    value_blocks = value_cache.reshape(seg_count, seg_width, kv_heads, HEAD_SIZE).astype(jnp.float32)
    scores = jnp.einsum('skgd,stkd->skgt', query_blocks, key_blocks) * HEAD_SIZE ** (-0.5)
    live_slots = jnp.arange(seg_width, dtype=jnp.int32)[None, None, None, :] < seg_lengths[:, None, None, None]
    scores = jnp.where(live_slots, scores, -jnp.inf)
    seg_max = lax.optimization_barrier(jnp.max(scores, axis=3))
    prob_rows = jnp.exp(scores - seg_max[..., None])
    seg_sum = lax.optimization_barrier(jnp.sum(prob_rows, axis=3))
    rounded = lax.optimization_barrier(prob_rows.astype(jnp.bfloat16)).astype(jnp.float32)
    seg_out = jnp.einsum('skgt,stkd->skgd', rounded, value_blocks)
    return (seg_max.reshape(seg_count, HQ), seg_sum.reshape(seg_count, HQ), seg_out.reshape(seg_count, HQ, HEAD_SIZE))

def reduce_rows(seg_max, seg_sum, seg_out, row_ids, row_count):
    row_max = jax.ops.segment_max(seg_max, row_ids, num_segments=row_count)
    weight = jnp.exp(seg_max - jnp.take(row_max, row_ids, axis=0))
    row_sum = jax.ops.segment_sum(seg_sum * weight, row_ids, num_segments=row_count)
    row_out = jax.ops.segment_sum(seg_out * weight[..., None], row_ids, num_segments=row_count)
    return (row_max, row_sum, row_out)

def fold_own(row_max, row_sum, row_out, query_own, kv_own):
    row_count = query_own.shape[0]
    kv_heads = kv_own.shape[2] // HEAD_SIZE
    group_size = HQ // kv_heads
    query_blocks = query_own.reshape(row_count, kv_heads, group_size, HEAD_SIZE).astype(jnp.float32)
    new_key = kv_own[:, 0].reshape(row_count, kv_heads, 1, HEAD_SIZE).astype(jnp.float32)
    new_value = kv_own[:, 1].reshape(row_count, kv_heads, 1, HEAD_SIZE).astype(jnp.float32)
    own_score = lax.optimization_barrier(jnp.sum(query_blocks * new_key, axis=3)).reshape(row_count, HQ) * HEAD_SIZE ** (-0.5)
    merged = jnp.maximum(row_max, own_score)
    old_weight = jnp.exp(row_max - merged)
    new_weight = jnp.exp(own_score - merged)
    total_sum = row_sum * old_weight + new_weight
    value_term = jnp.broadcast_to(new_value, (row_count, kv_heads, group_size, HEAD_SIZE)).reshape(row_count, HQ, HEAD_SIZE)
    merged_out = row_out * old_weight[..., None] + value_term * new_weight[..., None]
    return (merged, total_sum, merged_out)

def finish(row_max, row_sum, row_out):
    floored = jnp.maximum(row_sum, 1.0)
    block_lse = row_max + jnp.log(floored)
    block_share = (row_out / floored[..., None]).astype(jnp.bfloat16)
    return (block_lse, block_share)

def reference(hidden_in, queries, fresh_key_value, segment_key_cache, segment_value_cache, segment_owner_row, segment_length, expert_ids, gate_score, out_proj, norm_gain, w_gate, w_up, w_down):
    row_total = ROW_DEV * N_DEV

    def block_step(carry_state, block_data):
        best_lse, denominator, numerator = carry_state
        key_block, value_block, row_block, len_block, block_index = block_data
        own_first = (block_index * ROW_DEV).astype(jnp.int32)
        query_rows = jnp.take(queries, row_block, axis=0)
        seg_max, seg_sum, seg_out = segment_terms(query_rows, key_block, value_block, len_block)
        row_max, row_sum, row_out = reduce_rows(seg_max, seg_sum, seg_out, row_block, row_total)
        query_own = lax.dynamic_slice_in_dim(queries, own_first, ROW_DEV, 0)
        kv_own = lax.dynamic_slice_in_dim(fresh_key_value, own_first, ROW_DEV, 0)
        own_max, own_sum, own_out = fold_own(lax.dynamic_slice_in_dim(row_max, own_first, ROW_DEV, 0), lax.dynamic_slice_in_dim(row_sum, own_first, ROW_DEV, 0), lax.dynamic_slice_in_dim(row_out, own_first, ROW_DEV, 0), query_own, kv_own)
        row_max = lax.dynamic_update_slice_in_dim(row_max, own_max, own_first, 0)
        row_sum = lax.dynamic_update_slice_in_dim(row_sum, own_sum, own_first, 0)
        row_out = lax.dynamic_update_slice_in_dim(row_out, own_out, own_first, 0)
        block_lse, block_share = finish(row_max, row_sum, row_out)
        share_f32 = lax.optimization_barrier(block_share).astype(jnp.float32)
        fresh_max = jnp.maximum(best_lse, block_lse)
        old_weight = jnp.exp(best_lse - fresh_max)
        new_weight = jnp.exp(block_lse - fresh_max)
        return ((fresh_max, denominator * old_weight + new_weight, numerator * old_weight[..., None] + share_f32 * new_weight[..., None]), None)
    initial = (jnp.full((row_total, HQ), FLOOR_MAX, jnp.float32), jnp.zeros((row_total, HQ), jnp.float32), jnp.zeros((row_total, HQ, HEAD_SIZE), jnp.float32))
    layer_block_inputs = (segment_key_cache.reshape(N_DEV, DEVICE_SEGMENTS, SEGMENT_SLOTS, KEY_VALUE_HEADS * HEAD_SIZE), segment_value_cache.reshape(N_DEV, DEVICE_SEGMENTS, SEGMENT_SLOTS, KEY_VALUE_HEADS * HEAD_SIZE), segment_owner_row.reshape(N_DEV, DEVICE_SEGMENTS), segment_length.reshape(N_DEV, DEVICE_SEGMENTS), jnp.arange(N_DEV, dtype=jnp.int32))
    final_state, unused = lax.scan(block_step, initial, layer_block_inputs)
    attention = (final_state[2] / final_state[1][..., None]).astype(jnp.bfloat16).reshape(row_total, HQ * HEAD_SIZE)
    per_group = HPD * HEAD_SIZE
    attention_parts = attention.reshape(row_total, N_DEV, per_group).transpose(1, 0, 2)
    weight_parts = out_proj.reshape(N_DEV, per_group, D)

    def project_step(running, pair_items):
        group_part = jnp.dot(pair_items[0], pair_items[1], preferred_element_type=jnp.float32).astype(jnp.bfloat16)
        return (running + lax.optimization_barrier(group_part).astype(jnp.float32), None)
    projected, unused = lax.scan(project_step, jnp.zeros((row_total, D), jnp.float32), (attention_parts, weight_parts))
    mixed = (hidden_in.astype(jnp.float32) + projected).astype(jnp.bfloat16)
    mixed_f32 = mixed.astype(jnp.float32)
    normed = (mixed_f32 * lax.rsqrt(lax.optimization_barrier(jnp.mean(mixed_f32 * mixed_f32, axis=1, keepdims=True)) + 1e-06) * norm_gain.astype(jnp.float32)).astype(jnp.bfloat16)
    gate_probs = jnp.exp(gate_score.astype(jnp.float32) / 4.0)
    gate_probs = gate_probs / lax.optimization_barrier(jnp.sum(gate_probs, axis=1, keepdims=True))
    row_limit = N_DEV * CAP

    def expert_step(running, block_data):
        gate_weight, up_weight, down_weight, expert_index = block_data
        chosen = expert_ids == expert_index
        picked = jnp.any(chosen, axis=1)
        weight = lax.optimization_barrier(jnp.sum(jnp.where(chosen, gate_probs, 0.0), axis=1))
        row_order = jnp.argsort(jnp.where(picked, 0, 1).astype(jnp.int32), stable=True)[:row_limit].astype(jnp.int32)
        tokens = jnp.take(normed, row_order, axis=0)
        gate_proj = jnp.dot(tokens, gate_weight, preferred_element_type=jnp.float32)
        up_proj = jnp.dot(tokens, up_weight, preferred_element_type=jnp.float32)
        activated = (jax.nn.silu(gate_proj) * up_proj).astype(jnp.bfloat16)
        result = jnp.dot(activated, down_weight, preferred_element_type=jnp.float32).astype(jnp.bfloat16)
        result = lax.optimization_barrier(result).astype(jnp.float32)
        return (running.at[row_order].add(result * jnp.take(weight, row_order, axis=0)[:, None]), None)
    moe_sum, unused = lax.scan(expert_step, jnp.zeros((row_total, D), jnp.float32), (w_gate, w_up, w_down, jnp.arange(EXPERTS, dtype=jnp.int32)))
    return (mixed_f32 + moe_sum).astype(jnp.bfloat16)
```

```python
import functools

import jax
import jax.numpy as jnp
from jax import lax
from jax.experimental import pallas as pl
from jax.experimental.pallas import tpu as pltpu
from jax.sharding import PartitionSpec as P

HEAD_SIZE = 128
LANES = 128
NEG = -1e30
BF = jnp.bfloat16
F32 = jnp.float32


def xor_masks(devices):
    far = devices // 4
    return [c + 2 * y + 4 * z for c in range(2) for y in range(2) for z in range(far)]


def swap(x, mask, devices):
    return lax.ppermute(x, "dev", [(i, i ^ mask) for i in range(devices)])


def gather_blocks(x, devices):
    far = devices // 4
    z_order = sorted(range(1, far), reverse=True)
    z_parts = {0: x}
    for i in z_order:
        z_parts[i] = swap(x, 4 * i, devices)
    near = [z_parts[i] for i in range(far)]
    near = near + [swap(b, 2, devices) for b in near]
    return near + [swap(b, 1, devices) for b in near]


def scatter_blocks(x, devices):
    far = devices // 4
    parts = x.reshape((2, 2, far) + x.shape[1:])
    pieces = []
    for i in range(far - 1, -1, -1):
        pair = parts[0, :, i] + swap(parts[1, :, i], 1, devices)
        mine = pair[0] + swap(pair[1], 2, devices)
        pieces.append(swap(mine, 4 * i, devices) if i else mine)
    return pieces


def lane_pick(vec, lane_iota, index):
    return jnp.sum(jnp.where(lane_iota == index, vec, 0.0), axis=1, keepdims=True)


def attend_kernel(
    me_ref, owner_row_ref, owner_col_ref, bias_ref, k_ref, v_ref, *rest,
    devices, row_dev, width, q_heads, kv_heads, slots, seg_width,
):
    pieces = rest[:devices]
    out_ref, q_scr, o_scr, m_scr = rest[devices:]
    me = me_ref[0]
    masks = xor_masks(devices)
    rows = devices * row_dev
    segs = owner_row_ref.shape[1]
    hp = q_heads // devices
    per_kv = q_heads // kv_heads
    qk = q_heads * HEAD_SIZE
    ext = qk + 2 * kv_heads * HEAD_SIZE
    hots = []
    per_lane = LANES // row_dev
    lane = lax.broadcasted_iota(jnp.int32, (1, LANES), 1)
    for c in range(rows // LANES):
        gid = jnp.zeros((1, LANES), jnp.int32)
        for i in range(per_lane):
            base = (me ^ masks[c * per_lane + i]) * row_dev - i * row_dev
            gid = jnp.where(lane // row_dev == i, lane + base, gid)
        hots.append((owner_col_ref[...] == gid).astype(F32).astype(BF))
    hot = jnp.concatenate(hots, axis=1)
    step = 512
    for c in range(qk // step):
        block = jnp.concatenate([p[:, c * step : (c + 1) * step] for p in pieces], axis=0)
        q_scr[:, c * step : (c + 1) * step] = jnp.dot(
            hot, block, preferred_element_type=F32
        ).astype(BF)
    group = 16
    wide = group * seg_width
    r_i = lax.broadcasted_iota(jnp.int32, (group, wide), 0)
    c_i = lax.broadcasted_iota(jnp.int32, (group, wide), 1)
    eye_bias = jnp.where(r_i == c_i // seg_width, 0.0, NEG)
    ones = jnp.ones((wide, HEAD_SIZE), BF)
    stat_lanes = m_scr.shape[1]
    m_lane = lax.broadcasted_iota(jnp.int32, (group, stat_lanes), 1)
    for g in range(segs // group):
        bias = eye_bias + bias_ref[g : g + 1, :]
        m_acc = jnp.zeros((group, stat_lanes), F32)
        for kv in range(kv_heads):
            lo = kv * per_kv
            q_tile = jnp.concatenate(
                [
                    q_scr[g * group : (g + 1) * group, (lo + h) * HEAD_SIZE : (lo + h + 1) * HEAD_SIZE]
                    for h in range(per_kv)
                ],
                axis=0,
            )
            k_tile = k_ref[g * wide : (g + 1) * wide, kv * HEAD_SIZE : (kv + 1) * HEAD_SIZE]
            v_tile = v_ref[g * wide : (g + 1) * wide, kv * HEAD_SIZE : (kv + 1) * HEAD_SIZE]
            s = lax.dot_general(
                q_tile, k_tile, (((1,), (1,)), ((), ())), preferred_element_type=F32
            ) * HEAD_SIZE ** (-0.5)
            s = s.reshape(per_kv, group, wide) + bias[None]
            m = jnp.max(s, axis=2, keepdims=True)
            prob = jnp.exp(s - m).reshape(per_kv * group, wide).astype(BF)
            o = jnp.dot(prob, jnp.concatenate([v_tile, ones], axis=1), preferred_element_type=F32)
            o_scr[lo : lo + per_kv, g * group : (g + 1) * group, :] = o.reshape(
                per_kv, group, 2 * HEAD_SIZE
            ).astype(BF)
            for h in range(per_kv):
                m_acc = jnp.where(m_lane == lo + h, m[h], m_acc)
        m_scr[g * group : (g + 1) * group, :] = m_acc
    m_t = m_scr[...].T
    ext_sum = jnp.zeros((1, LANES), F32)
    for p in range(devices):
        vec = pieces[p][0:1, ext : ext + LANES].astype(F32)
        ext_sum = ext_sum + jnp.where((me ^ masks[p]) == me - 1, vec, 0.0)
    prev_last = 16.0 * lane_pick(ext_sum, lane, 18) + lane_pick(ext_sum, lane, 19)
    owner = owner_row_ref[...]
    first = jnp.min(owner.astype(F32), axis=1, keepdims=True)
    repeated = jnp.logical_and(first == prev_last, me > 0)
    slot = jnp.where(
        jnp.logical_and(owner.astype(F32) == first, repeated), rows + me, owner
    )
    mask = lax.broadcasted_iota(jnp.int32, (slots, segs), 0) == slot
    stats = devices * 8
    st_lane = lax.broadcasted_iota(jnp.int32, (slots, stats), 1)
    max_acc = jnp.zeros((slots, stats), F32)
    sum_acc = jnp.ones((slots, stats), F32)
    for d in range(devices):
        pos_mask = me ^ d
        far = devices // 4
        pos = (pos_mask & 1) * (2 * far) + ((pos_mask >> 1) & 1) * far + (pos_mask >> 2)
        for hh in range(hp):
            h = d * hp + hh
            m_row = m_t[h : h + 1, :]
            mm = jnp.where(mask, m_row, NEG)
            r_max = jnp.maximum(jnp.max(mm, axis=1, keepdims=True), 0.1 * NEG)
            weight = jnp.exp(mm - r_max).astype(BF)
            r = jnp.dot(weight, o_scr[h], preferred_element_type=F32)
            r_sum = jnp.maximum(r[:, HEAD_SIZE:], 1.0)
            out_ref[pos, 0:slots, hh * HEAD_SIZE : (hh + 1) * HEAD_SIZE] = (
                r[:, :HEAD_SIZE] / r_sum
            ).astype(BF)
            here = jnp.zeros((slots, stats), jnp.bool_)
            for part in range(3):
                here = jnp.logical_or(here, st_lane == d * 8 + part * hp + hh)
            max_acc = jnp.where(here, r_max, max_acc)
            sum_acc = jnp.where(here, r_sum[:, 0:1], sum_acc)
    owned = jnp.max(jnp.where(mask, 1.0, 0.0), axis=1, keepdims=True)
    lse = jnp.where(owned > 0.0, max_acc + jnp.log(sum_acc), 0.0)
    hi = lse.astype(BF).astype(F32)
    rest1 = lse - hi
    mid = rest1.astype(BF).astype(F32)
    low = rest1 - mid
    part = (st_lane % 8) // hp
    lse = jnp.where(part == 0, hi, jnp.where(part == 1, mid, low))
    pad = -(-slots // width) * width - slots
    pad_t = -(-slots // LANES) * LANES - slots
    if pad_t:
        lse = jnp.concatenate([lse, jnp.zeros((pad_t, stats), F32)], axis=0)
    lse_t = lse.T
    if pad > pad_t:
        lse_t = jnp.concatenate([lse_t, jnp.zeros((stats, pad - pad_t), F32)], axis=1)
    tail = out_ref.shape[1] - slots
    for d in range(devices):
        pos_mask = me ^ d
        far = devices // 4
        pos = (pos_mask & 1) * (2 * far) + ((pos_mask >> 1) & 1) * far + (pos_mask >> 2)
        strips = [
            lse_t[d * 8 : (d + 1) * 8, b * width : (b + 1) * width]
            for b in range((slots + pad) // width)
        ]
        if len(strips) * 8 < tail:
            strips.append(jnp.zeros((tail - len(strips) * 8, width), F32))
        out_ref[pos, slots:, :] = jnp.concatenate(strips, axis=0).astype(BF)


def combine_kernel(
    me_ref, w_ref, *rest, devices, row_dev, width, q_heads, kv_heads, slots,
):
    pieces = rest[:devices]
    far = devices // 4
    shares = rest[devices : devices + far]
    out_ref, x_scr, l_scr = rest[devices + far :]
    me = me_ref[0]
    masks = xor_masks(devices)
    rows = devices * row_dev
    hp = q_heads // devices
    qk = q_heads * HEAD_SIZE
    ext = qk + 2 * kv_heads * HEAD_SIZE
    total = shares[0][...].astype(F32)
    for s in shares[1:]:
        total = total + s[...].astype(F32)
    x_scr[...] = total
    strips = -(-slots // width)
    lse8 = jnp.concatenate(
        [total[slots + 8 * b : slots + 8 * (b + 1), :] for b in range(strips)], axis=1
    )
    lse_rows = [
        lse8[hh : hh + 1, :] + lse8[hp + hh : hp + hh + 1, :] + lse8[2 * hp + hh : 2 * hp + hh + 1, :]
        for hh in range(hp)
    ]
    head_pos = lax.broadcasted_iota(jnp.int32, (LANES, rows), 0)
    spread = jnp.zeros((LANES, rows), F32)
    for hh in range(hp):
        spread = jnp.where(head_pos == hh, lse_rows[hh][:, :rows], spread)
    l_scr[...] = spread.T
    lane = lax.broadcasted_iota(jnp.int32, (1, LANES), 1)
    first = jnp.full((1, LANES), -1.0, F32)
    before = jnp.full((1, LANES), -2.0, F32)
    for p in range(devices):
        vec = pieces[p][0:1, ext : ext + LANES].astype(F32)
        dev = me ^ masks[p]
        first = jnp.where(
            lane == dev, 16.0 * lane_pick(vec, lane, 16) + lane_pick(vec, lane, 17), first
        )
        before = jnp.where(
            lane == dev + 1, 16.0 * lane_pick(vec, lane, 18) + lane_pick(vec, lane, 19), before
        )
    again = jnp.where(jnp.logical_and(first == before, lane < devices), first, -1.0).astype(jnp.int32)
    row_id = jnp.concatenate(
        [
            lax.broadcasted_iota(jnp.int32, (row_dev, LANES), 0) + (me ^ masks[p]) * row_dev
            for p in range(devices)
        ],
        axis=0,
    )
    share = jnp.concatenate(
        [x_scr[pl.ds((me ^ masks[p]) * row_dev, row_dev), :] for p in range(devices)], axis=0
    )
    lse_col = jnp.concatenate(
        [l_scr[pl.ds((me ^ masks[p]) * row_dev, row_dev), :] for p in range(devices)], axis=0
    )
    kv = (me * hp) // (q_heads // kv_heads)
    q_at = pl.multiple_of(me * width, LANES)
    k_at = pl.multiple_of(qk + kv * HEAD_SIZE, LANES)
    v_at = pl.multiple_of(qk + (kv_heads + kv) * HEAD_SIZE, LANES)
    q = jnp.concatenate([p[:, pl.ds(q_at, width)] for p in pieces], axis=0).astype(F32)
    key = jnp.concatenate([p[:, pl.ds(k_at, HEAD_SIZE)] for p in pieces], axis=0).astype(F32)
    val = jnp.concatenate([p[:, pl.ds(v_at, HEAD_SIZE)] for p in pieces], axis=0).astype(F32)
    chosen = row_id == again
    heads = []
    for hh in range(hp):
        cut = slice(hh * HEAD_SIZE, (hh + 1) * HEAD_SIZE)
        own = jnp.sum(q[:, cut] * key, axis=1, keepdims=True) * HEAD_SIZE ** (-0.5)
        lse_p = lse_col[:, hh : hh + 1]
        extra = jnp.where(chosen, lse_rows[hh][:, rows : rows + LANES], NEG)
        top = jnp.maximum(jnp.maximum(lse_p, own), jnp.max(extra, axis=1, keepdims=True))
        w_p = jnp.exp(lse_p - top)
        w_o = jnp.exp(own - top)
        w_e = jnp.exp(extra - top)
        more = jnp.concatenate(
            [x_scr[rows:slots, cut], jnp.zeros((LANES - devices, HEAD_SIZE), F32)], axis=0
        )
        num = w_p * share[:, cut] + w_o * val + jnp.dot(
            w_e, more, precision=lax.Precision.HIGHEST, preferred_element_type=F32
        )
        den = w_p + w_o + jnp.sum(w_e, axis=1, keepdims=True)
        heads.append((num / den).astype(BF))
    attn = heads[0] if hp == 1 else jnp.concatenate(heads, axis=1)
    step = 1024
    for c in range(w_ref.shape[1] // step):
        cut = slice(c * step, (c + 1) * step)
        r = jnp.dot(attn, w_ref[:, cut], preferred_element_type=F32).astype(BF)
        for p in range(devices):
            out_ref[p, :, cut] = r[p * row_dev : (p + 1) * row_dev]


def expert_kernel(me_ref, *rest, devices, row_dev, top):
    pieces = rest[:devices]
    ext = rest[devices : 2 * devices]
    gate_ref, up_ref, down_ref, out_ref, x_scr, acc = rest[2 * devices :]
    i = pl.program_id(0)

    @pl.when(i == 0)
    def _():
        for p in range(devices):
            x_scr[p * row_dev : (p + 1) * row_dev, :] = pieces[p][...]
        acc[...] = jnp.zeros(acc.shape, F32)

    x = x_scr[...]
    a = jnp.dot(x, gate_ref[...], preferred_element_type=F32)
    b = jnp.dot(x, up_ref[...], preferred_element_type=F32)
    h = (a / (1.0 + jnp.exp(-a)) * b).astype(BF)
    acc[...] += jnp.dot(h, down_ref[...], preferred_element_type=F32)

    @pl.when(i == pl.num_programs(0) - 1)
    def _():
        me = me_ref[0]
        lane = lax.broadcasted_iota(jnp.int32, (row_dev, LANES), 1)
        for p in range(devices):
            e = ext[p][...].astype(F32)
            score = jnp.where(jnp.logical_and(lane >= top, lane < 2 * top), jnp.exp(e * 0.25), 0.0)
            total = jnp.sum(score, axis=1, keepdims=True)
            weight = jnp.zeros((row_dev, 1), F32)
            for k in range(top):
                weight = weight + jnp.where(
                    e[:, k : k + 1] == me.astype(F32), score[:, top + k : top + k + 1], 0.0
                )
            weight = weight / total
            y = acc[p * row_dev : (p + 1) * row_dev, :].astype(BF).astype(F32)
            out_ref[p] = (y * weight).astype(BF)


def on_device(
    hidden_in, queries, fresh_key_value, segment_key_cache, segment_value_cache,
    segment_owner_row, segment_length, expert_ids, gate_score, out_proj, norm_gain,
    w_gate, w_up, w_down,
):
    devices = lax.axis_size("dev")
    me = lax.axis_index("dev").astype(jnp.int32).reshape(1)
    row_dev, d_model = hidden_in.shape
    rows = row_dev * devices
    q_heads = queries.shape[1] // HEAD_SIZE
    kv_heads = fresh_key_value.shape[2] // HEAD_SIZE
    segs, seg_width = segment_key_cache.shape[:2]
    top = expert_ids.shape[1]
    width = out_proj.shape[0]
    slots = rows + devices
    strips = -(-slots // width)
    tall = slots + -(-strips // 2) * 16
    first = segment_owner_row[0]
    last = segment_owner_row[segs - 1]
    ends = jnp.stack([first // 16, first % 16, last // 16, last % 16]).astype(BF)
    extra = jnp.concatenate(
        [
            expert_ids.astype(BF),
            gate_score.astype(BF),
            jnp.broadcast_to(ends[None], (row_dev, 4)),
            jnp.zeros((row_dev, LANES - 2 * top - 4), BF),
        ],
        axis=1,
    )
    payload = jnp.concatenate(
        [queries, fresh_key_value.reshape(row_dev, -1), extra], axis=1
    )
    group = 16
    slot_ids = jnp.arange(seg_width, dtype=jnp.int32)
    bias = jnp.where(slot_ids[None] < segment_length[:, None], 0.0, NEG).astype(F32)
    bias = bias.reshape(segs // group, group * seg_width)
    owner_row = segment_owner_row.reshape(1, segs)
    owner_col = jnp.broadcast_to(segment_owner_row[:, None], (segs, LANES))
    pieces = gather_blocks(payload, devices)
    smem = pl.BlockSpec(memory_space=pltpu.SMEM)
    vmem = pl.BlockSpec(memory_space=pltpu.VMEM)
    stat_lanes = LANES
    params = pltpu.CompilerParams(vmem_limit_bytes=56 * 1024 * 1024)
    table = pl.pallas_call(
        functools.partial(
            attend_kernel, devices=devices, row_dev=row_dev, width=width, q_heads=q_heads,
            kv_heads=kv_heads, slots=slots, seg_width=seg_width,
        ),
        out_shape=jax.ShapeDtypeStruct((devices, tall, width), BF),
        in_specs=[smem] + [vmem] * (5 + devices),
        out_specs=vmem,
        scratch_shapes=[
            pltpu.VMEM((segs, q_heads * HEAD_SIZE), BF),
            pltpu.VMEM((q_heads, segs, 2 * HEAD_SIZE), BF),
            pltpu.VMEM((segs, stat_lanes), F32),
        ],
        compiler_params=params,
        name="attend",
    )(
        me, owner_row, owner_col, bias,
        segment_key_cache.reshape(segs * seg_width, -1),
        segment_value_cache.reshape(segs * seg_width, -1),
        *pieces,
    )
    shares = scatter_blocks(table, devices)
    part = pl.pallas_call(
        functools.partial(
            combine_kernel, devices=devices, row_dev=row_dev, width=width, q_heads=q_heads,
            kv_heads=kv_heads, slots=slots,
        ),
        out_shape=jax.ShapeDtypeStruct((devices, row_dev, d_model), BF),
        in_specs=[smem] + [vmem] * (1 + devices + devices // 4),
        out_specs=vmem,
        scratch_shapes=[pltpu.VMEM((tall, width), F32), pltpu.VMEM((rows, LANES), F32)],
        compiler_params=params,
        name="combine",
    )(me, out_proj, *pieces, *shares)
    projected = sum(p.astype(F32) for p in scatter_blocks(part, devices))
    mixed = (hidden_in.astype(F32) + projected).astype(BF).astype(F32)
    normed = (
        mixed
        * lax.rsqrt(jnp.mean(mixed * mixed, axis=1, keepdims=True) + 1e-06)
        * norm_gain.astype(F32)
    ).astype(BF)
    tokens = gather_blocks(normed, devices)
    ff = w_gate.shape[2]
    tile = 256
    ext_at = (q_heads + 2 * kv_heads) * HEAD_SIZE // LANES
    moe = pl.pallas_call(
        functools.partial(expert_kernel, devices=devices, row_dev=row_dev, top=top),
        grid=(ff // tile,),
        out_shape=jax.ShapeDtypeStruct((devices, row_dev, d_model), BF),
        in_specs=[smem]
        + [pl.BlockSpec((row_dev, d_model), lambda i: (0, 0))] * devices
        + [pl.BlockSpec((row_dev, LANES), lambda i: (0, ext_at))] * devices
        + [
            pl.BlockSpec((None, d_model, tile), lambda i: (0, 0, i)),
            pl.BlockSpec((None, d_model, tile), lambda i: (0, 0, i)),
            pl.BlockSpec((None, tile, d_model), lambda i: (0, i, 0)),
        ],
        out_specs=pl.BlockSpec((devices, row_dev, d_model), lambda i: (0, 0, 0)),
        scratch_shapes=[pltpu.VMEM((rows, d_model), BF), pltpu.VMEM((rows, d_model), F32)],
        compiler_params=params,
        name="experts",
    )(me, *tokens, *pieces, w_gate, w_up, w_down)
    summed = sum(p.astype(F32) for p in scatter_blocks(moe, devices))
    return (mixed + summed).astype(BF)


def solution(mesh):
    both = ("groups", "dev")
    placed = (
        P(both, None), P(both, None), P(both, None, None), P(both, None, None),
        P(both, None, None), P(both), P(both), P(both, None), P(both, None),
        P("dev", None), P(), P("dev", None, None), P("dev", None, None), P("dev", None, None),
    )
    return jax.shard_map(
        on_device, mesh=mesh, in_specs=placed, out_specs=P(both, None), check_vma=False
    )
```

```python
import functools

import jax
import jax.numpy as jnp
from jax import lax
from jax.experimental import pallas as pl
from jax.experimental.pallas import tpu as pltpu
from jax.sharding import PartitionSpec as P

HEAD_SIZE = 128
LANES = 128
NEG = -1e30
BF = jnp.bfloat16
F32 = jnp.float32


def xor_masks(devices):
    far = devices // 4
    return [c + 2 * y + 4 * z for c in range(2) for y in range(2) for z in range(far)]


def swap(x, mask, devices):
    return lax.ppermute(x, "dev", [(i, i ^ mask) for i in range(devices)])


def gather_blocks(x, devices):
    far = devices // 4
    z_order = sorted(range(1, far), reverse=True)
    z_parts = {0: x}
    for i in z_order:
        z_parts[i] = swap(x, 4 * i, devices)
    near = [z_parts[i] for i in range(far)]
    near = near + [swap(b, 2, devices) for b in near]
    return near + [swap(b, 1, devices) for b in near]


def scatter_blocks(keep, send, devices):
    pieces = []
    for i in range(devices // 4 - 1, -1, -1):
        pair = keep[i] + swap(send[i], 1, devices)
        mine = pair[0] + swap(pair[1], 2, devices)
        pieces.append(swap(mine, 4 * i, devices) if i else mine)
    return pieces


def split_shapes(devices, tail):
    return [jax.ShapeDtypeStruct((2,) + tail, BF)] * (devices // 2)


def split_refs(refs, devices):
    far = devices // 4
    return [(refs[c * far + z], y) for c in range(2) for y in range(2) for z in range(far)]


def lane_pick(vec, lane_iota, index):
    return jnp.sum(jnp.where(lane_iota == index, vec, 0.0), axis=1, keepdims=True)


def payload_kernel(q_ref, fresh_ref, ids_ref, score_ref, owner_ref, out_ref, *, top):
    row_dev, qk = q_ref.shape
    kv = fresh_ref.shape[2]
    out_ref[:, :qk] = q_ref[...]
    out_ref[:, qk : qk + kv] = fresh_ref[:, 0, :]
    out_ref[:, qk + kv : qk + 2 * kv] = fresh_ref[:, 1, :]
    segs = owner_ref.shape[1]
    owner = owner_ref[...]
    first = jnp.broadcast_to(owner[:, 0:1], (row_dev, LANES))
    last = jnp.broadcast_to(owner[:, segs - 1 : segs], (row_dev, LANES))
    lane = lax.broadcasted_iota(jnp.int32, (row_dev, LANES), 1)
    extra = jnp.zeros((row_dev, LANES), jnp.int32)
    for k in range(top):
        extra = jnp.where(lane == k, ids_ref[:, k : k + 1], extra)
        extra = jnp.where(lane == top + k, score_ref[:, k : k + 1], extra)
    for k, v in enumerate((first // 16, first % 16, last // 16, last % 16)):
        extra = jnp.where(lane == 2 * top + k, v, extra)
    out_ref[:, qk + 2 * kv :] = extra.astype(F32).astype(BF)


def attend_kernel(
    me_ref, owner_row_ref, length_ref, k_ref, v_ref, *rest,
    devices, row_dev, width, q_heads, kv_heads, slots, seg_width,
):
    pieces = rest[:devices]
    outs = split_refs(rest[devices : devices + devices // 2], devices)
    q_scr, o_scr, m_scr, t_scr, l_scr = rest[devices + devices // 2 :]
    me = me_ref[0]
    masks = xor_masks(devices)
    rows = devices * row_dev
    segs = owner_row_ref.shape[1]
    hp = q_heads // devices
    per_kv = q_heads // kv_heads
    qk = q_heads * HEAD_SIZE
    ext = qk + 2 * kv_heads * HEAD_SIZE
    owner_col = jnp.broadcast_to(owner_row_ref[...].astype(F32), (LANES, segs)).T.astype(jnp.int32)
    hots = []
    per_lane = LANES // row_dev
    lane = lax.broadcasted_iota(jnp.int32, (1, LANES), 1)
    for c in range(rows // LANES):
        gid = jnp.zeros((1, LANES), jnp.int32)
        for i in range(per_lane):
            base = (me ^ masks[c * per_lane + i]) * row_dev - i * row_dev
            gid = jnp.where(lane // row_dev == i, lane + base, gid)
        hots.append((owner_col == gid).astype(F32).astype(BF))
    hot = jnp.concatenate(hots, axis=1)
    step = 512
    for c in range(qk // step):
        block = jnp.concatenate([p[:, c * step : (c + 1) * step] for p in pieces], axis=0)
        q_scr[:, c * step : (c + 1) * step] = jnp.dot(
            hot, block, preferred_element_type=F32
        ).astype(BF)
    group = 16
    wide = group * seg_width
    r_i = lax.broadcasted_iota(jnp.int32, (group, wide), 0)
    c_i = lax.broadcasted_iota(jnp.int32, (group, wide), 1)
    eye_bias = jnp.where(r_i == c_i // seg_width, 0.0, NEG)
    ones = jnp.ones((wide, HEAD_SIZE), BF)
    of_group = lax.broadcasted_iota(jnp.int32, (segs // group, segs), 1) // group
    g_i = lax.broadcasted_iota(jnp.int32, (segs // group, segs), 0)
    lens = jnp.where(of_group == g_i, length_ref[...], 0).astype(F32).astype(BF)
    e_i = lax.broadcasted_iota(jnp.int32, (segs, wide), 0) % group
    e_j = lax.broadcasted_iota(jnp.int32, (segs, wide), 1) // seg_width
    spread = jnp.where(e_i == e_j, 1.0, 0.0).astype(BF)
    live = jnp.dot(lens, spread, preferred_element_type=F32)
    at = (lax.broadcasted_iota(jnp.int32, (segs // group, wide), 1) % seg_width).astype(F32)
    live_bias = jnp.where(at < live, 0.0, NEG)
    stat_lanes = m_scr.shape[1]
    m_lane = lax.broadcasted_iota(jnp.int32, (group, stat_lanes), 1)
    for g in range(segs // group):
        bias = eye_bias + live_bias[g : g + 1, :]
        m_acc = jnp.zeros((group, stat_lanes), F32)
        for kv in range(kv_heads):
            lo = kv * per_kv
            q_tile = jnp.concatenate(
                [
                    q_scr[g * group : (g + 1) * group, (lo + h) * HEAD_SIZE : (lo + h + 1) * HEAD_SIZE]
                    for h in range(per_kv)
                ],
                axis=0,
            )
            k_tile = k_ref[g * wide : (g + 1) * wide, kv * HEAD_SIZE : (kv + 1) * HEAD_SIZE]
            v_tile = v_ref[g * wide : (g + 1) * wide, kv * HEAD_SIZE : (kv + 1) * HEAD_SIZE]
            s = lax.dot_general(
                q_tile, k_tile, (((1,), (1,)), ((), ())), preferred_element_type=F32
            ) * HEAD_SIZE ** (-0.5)
            s = s.reshape(per_kv, group, wide) + bias[None]
            m = jnp.max(s, axis=2, keepdims=True)
            prob = jnp.exp(s - m).reshape(per_kv * group, wide).astype(BF)
            o = jnp.dot(prob, jnp.concatenate([v_tile, ones], axis=1), preferred_element_type=F32)
            o_scr[lo : lo + per_kv, g * group : (g + 1) * group, :] = o.reshape(
                per_kv, group, 2 * HEAD_SIZE
            ).astype(BF)
            for h in range(per_kv):
                m_acc = jnp.where(m_lane == lo + h, m[h], m_acc)
        m_scr[g * group : (g + 1) * group, :] = m_acc
    t_scr[...] = m_scr[...].T
    ext_sum = jnp.zeros((1, LANES), F32)
    for p in range(devices):
        vec = pieces[p][0:1, ext : ext + LANES].astype(F32)
        ext_sum = ext_sum + jnp.where((me ^ masks[p]) == me - 1, vec, 0.0)
    prev_last = 16.0 * lane_pick(ext_sum, lane, 18) + lane_pick(ext_sum, lane, 19)
    owner = owner_row_ref[...]
    first = jnp.min(owner.astype(F32), axis=1, keepdims=True)
    repeated = jnp.logical_and(first == prev_last, me > 0)
    slot = jnp.where(
        jnp.logical_and(owner.astype(F32) == first, repeated), rows + me, owner
    )
    mask = lax.broadcasted_iota(jnp.int32, (slots, segs), 0) == slot
    stats = devices * 8
    st_lane = lax.broadcasted_iota(jnp.int32, (slots, stats), 1)
    max_acc = jnp.zeros((slots, stats), F32)
    sum_acc = jnp.ones((slots, stats), F32)
    for p in range(devices):
        d = me ^ masks[p]
        out_ref, y = outs[p]
        for hh in range(hp):
            h = d * hp + hh
            m_row = t_scr[pl.ds(h, 1), :]
            mm = jnp.where(mask, m_row, NEG)
            r_max = jnp.maximum(jnp.max(mm, axis=1, keepdims=True), 0.1 * NEG)
            weight = jnp.exp(mm - r_max).astype(BF)
            r = jnp.dot(weight, o_scr[h], preferred_element_type=F32)
            r_sum = jnp.maximum(r[:, HEAD_SIZE:], 1.0)
            out_ref[y, 0:slots, hh * HEAD_SIZE : (hh + 1) * HEAD_SIZE] = (
                r[:, :HEAD_SIZE] / r_sum
            ).astype(BF)
            here = jnp.zeros((slots, stats), jnp.bool_)
            for part in range(3):
                here = jnp.logical_or(here, st_lane == d * 8 + part * hp + hh)
            max_acc = jnp.where(here, r_max, max_acc)
            sum_acc = jnp.where(here, r_sum[:, 0:1], sum_acc)
    owned = jnp.max(jnp.where(mask, 1.0, 0.0), axis=1, keepdims=True)
    lse = jnp.where(owned > 0.0, max_acc + jnp.log(sum_acc), 0.0)
    hi = lse.astype(BF).astype(F32)
    rest1 = lse - hi
    mid = rest1.astype(BF).astype(F32)
    low = rest1 - mid
    part = (st_lane % 8) // hp
    lse = jnp.where(part == 0, hi, jnp.where(part == 1, mid, low))
    pad = -(-slots // width) * width - slots
    pad_t = -(-slots // LANES) * LANES - slots
    if pad_t:
        lse = jnp.concatenate([lse, jnp.zeros((pad_t, stats), F32)], axis=0)
    lse_t = lse.T
    if pad > pad_t:
        lse_t = jnp.concatenate([lse_t, jnp.zeros((stats, pad - pad_t), F32)], axis=1)
    l_scr[...] = lse_t
    tail = outs[0][0].shape[1] - slots
    for p in range(devices):
        at = pl.multiple_of((me ^ masks[p]) * 8, 8)
        out_ref, y = outs[p]
        strips = [
            l_scr[pl.ds(at, 8), b * width : (b + 1) * width]
            for b in range((slots + pad) // width)
        ]
        if len(strips) * 8 < tail:
            strips.append(jnp.zeros((tail - len(strips) * 8, width), F32))
        out_ref[y, slots:, :] = jnp.concatenate(strips, axis=0).astype(BF)


def combine_kernel(
    me_ref, w_ref, *rest, devices, row_dev, width, q_heads, kv_heads, slots,
):
    pieces = rest[:devices]
    far = devices // 4
    shares = rest[devices : devices + far]
    outs = split_refs(rest[devices + far : devices + far + devices // 2], devices)
    x_scr, l_scr = rest[devices + far + devices // 2 :]
    me = me_ref[0]
    masks = xor_masks(devices)
    rows = devices * row_dev
    hp = q_heads // devices
    qk = q_heads * HEAD_SIZE
    ext = qk + 2 * kv_heads * HEAD_SIZE
    total = shares[0][...].astype(F32)
    for s in shares[1:]:
        total = total + s[...].astype(F32)
    x_scr[...] = total
    strips = -(-slots // width)
    lse8 = jnp.concatenate(
        [total[slots + 8 * b : slots + 8 * (b + 1), :] for b in range(strips)], axis=1
    )
    lse_rows = [
        lse8[hh : hh + 1, :] + lse8[hp + hh : hp + hh + 1, :] + lse8[2 * hp + hh : 2 * hp + hh + 1, :]
        for hh in range(hp)
    ]
    head_pos = lax.broadcasted_iota(jnp.int32, (LANES, rows), 0)
    spread = jnp.zeros((LANES, rows), F32)
    for hh in range(hp):
        spread = jnp.where(head_pos == hh, lse_rows[hh][:, :rows], spread)
    l_scr[...] = spread.T
    lane = lax.broadcasted_iota(jnp.int32, (1, LANES), 1)
    first = jnp.full((1, LANES), -1.0, F32)
    before = jnp.full((1, LANES), -2.0, F32)
    for p in range(devices):
        vec = pieces[p][0:1, ext : ext + LANES].astype(F32)
        dev = me ^ masks[p]
        first = jnp.where(
            lane == dev, 16.0 * lane_pick(vec, lane, 16) + lane_pick(vec, lane, 17), first
        )
        before = jnp.where(
            lane == dev + 1, 16.0 * lane_pick(vec, lane, 18) + lane_pick(vec, lane, 19), before
        )
    again = jnp.where(jnp.logical_and(first == before, lane < devices), first, -1.0).astype(jnp.int32)
    row_id = jnp.concatenate(
        [
            lax.broadcasted_iota(jnp.int32, (row_dev, LANES), 0) + (me ^ masks[p]) * row_dev
            for p in range(devices)
        ],
        axis=0,
    )
    share = jnp.concatenate(
        [x_scr[pl.ds((me ^ masks[p]) * row_dev, row_dev), :] for p in range(devices)], axis=0
    )
    lse_col = jnp.concatenate(
        [l_scr[pl.ds((me ^ masks[p]) * row_dev, row_dev), :] for p in range(devices)], axis=0
    )
    kv = (me * hp) // (q_heads // kv_heads)
    q_at = pl.multiple_of(me * width, LANES)
    k_at = pl.multiple_of(qk + kv * HEAD_SIZE, LANES)
    v_at = pl.multiple_of(qk + (kv_heads + kv) * HEAD_SIZE, LANES)
    q = jnp.concatenate([p[:, pl.ds(q_at, width)] for p in pieces], axis=0).astype(F32)
    key = jnp.concatenate([p[:, pl.ds(k_at, HEAD_SIZE)] for p in pieces], axis=0).astype(F32)
    val = jnp.concatenate([p[:, pl.ds(v_at, HEAD_SIZE)] for p in pieces], axis=0).astype(F32)
    chosen = row_id == again
    heads = []
    for hh in range(hp):
        cut = slice(hh * HEAD_SIZE, (hh + 1) * HEAD_SIZE)
        own = jnp.sum(q[:, cut] * key, axis=1, keepdims=True) * HEAD_SIZE ** (-0.5)
        lse_p = lse_col[:, hh : hh + 1]
        extra = jnp.where(chosen, lse_rows[hh][:, rows : rows + LANES], NEG)
        top = jnp.maximum(jnp.maximum(lse_p, own), jnp.max(extra, axis=1, keepdims=True))
        w_p = jnp.exp(lse_p - top)
        w_o = jnp.exp(own - top)
        w_e = jnp.exp(extra - top)
        more = jnp.concatenate(
            [x_scr[rows:slots, cut], jnp.zeros((LANES - devices, HEAD_SIZE), F32)], axis=0
        )
        num = w_p * share[:, cut] + w_o * val + jnp.dot(
            w_e, more, precision=lax.Precision.HIGHEST, preferred_element_type=F32
        )
        den = w_p + w_o + jnp.sum(w_e, axis=1, keepdims=True)
        heads.append((num / den).astype(BF))
    attn = heads[0] if hp == 1 else jnp.concatenate(heads, axis=1)
    step = 1024
    for c in range(w_ref.shape[1] // step):
        cut = slice(c * step, (c + 1) * step)
        r = jnp.dot(attn, w_ref[:, cut], preferred_element_type=F32).astype(BF)
        for p in range(devices):
            out_ref, y = outs[p]
            out_ref[y, :, cut] = r[p * row_dev : (p + 1) * row_dev]


def expert_kernel(me_ref, gate_ref, up_ref, down_ref, *rest, devices, row_dev, top, ext_at):
    pieces = rest[:devices]
    ext = rest[devices : 2 * devices]
    outs = split_refs(rest[2 * devices : 2 * devices + devices // 2], devices)
    x_scr, h_scr = rest[2 * devices + devices // 2 :]
    for p in range(devices):
        x_scr[p * row_dev : (p + 1) * row_dev, :] = pieces[p][...]
    ff = gate_ref.shape[2]
    d_model = gate_ref.shape[1]
    tile = 256
    for c in range(ff // tile):
        cut = slice(c * tile, (c + 1) * tile)
        a = jnp.dot(x_scr[...], gate_ref[0, :, cut], preferred_element_type=F32)
        b = jnp.dot(x_scr[...], up_ref[0, :, cut], preferred_element_type=F32)
        h_scr[:, cut] = (a / (1.0 + jnp.exp(-a)) * b).astype(BF)
    me = me_ref[0].astype(F32)
    lane = lax.broadcasted_iota(jnp.int32, (row_dev, LANES), 1)
    weights = []
    for p in range(devices):
        e = ext[p][:, ext_at : ext_at + LANES].astype(F32)
        score = jnp.where(jnp.logical_and(lane >= top, lane < 2 * top), jnp.exp(e * 0.25), 0.0)
        total = jnp.sum(score, axis=1, keepdims=True)
        weight = jnp.zeros((row_dev, 1), F32)
        for k in range(top):
            weight = weight + jnp.where(e[:, k : k + 1] == me, score[:, top + k : top + k + 1], 0.0)
        weights.append(weight / total)
    weight = jnp.concatenate(weights, axis=0)
    step = 512
    for c in range(d_model // step):
        cut = slice(c * step, (c + 1) * step)
        y = jnp.dot(h_scr[...], down_ref[0, :, cut], preferred_element_type=F32)
        y = (y.astype(BF).astype(F32) * weight).astype(BF)
        for p in range(devices):
            out_ref, side = outs[p]
            out_ref[side, :, cut] = y[p * row_dev : (p + 1) * row_dev]


def on_device(
    hidden_in, queries, fresh_key_value, segment_key_cache, segment_value_cache,
    segment_owner_row, segment_length, expert_ids, gate_score, out_proj, norm_gain,
    w_gate, w_up, w_down,
):
    devices = lax.axis_size("dev")
    me = lax.axis_index("dev").astype(jnp.int32).reshape(1)
    row_dev, d_model = hidden_in.shape
    rows = row_dev * devices
    q_heads = queries.shape[1] // HEAD_SIZE
    kv_heads = fresh_key_value.shape[2] // HEAD_SIZE
    segs, seg_width = segment_key_cache.shape[:2]
    top = expert_ids.shape[1]
    width = out_proj.shape[0]
    slots = rows + devices
    strips = -(-slots // width)
    tall = slots + -(-strips // 2) * 16
    smem = pl.BlockSpec(memory_space=pltpu.SMEM)
    vmem = pl.BlockSpec(memory_space=pltpu.VMEM)
    half = devices // 2
    far = devices // 4
    owner_row = segment_owner_row.reshape(1, segs)
    ext_at = (q_heads + 2 * kv_heads) * HEAD_SIZE
    payload = pl.pallas_call(
        functools.partial(payload_kernel, top=top),
        out_shape=jax.ShapeDtypeStruct((row_dev, ext_at + LANES), BF),
        in_specs=[vmem] * 5,
        out_specs=vmem,
        name="payload",
    )(queries, fresh_key_value, expert_ids, gate_score, owner_row)
    pieces = gather_blocks(payload, devices)
    params = pltpu.CompilerParams(vmem_limit_bytes=24 * 1024 * 1024)
    stats = devices * 8
    table = pl.pallas_call(
        functools.partial(
            attend_kernel, devices=devices, row_dev=row_dev, width=width, q_heads=q_heads,
            kv_heads=kv_heads, slots=slots, seg_width=seg_width,
        ),
        out_shape=split_shapes(devices, (tall, width)),
        in_specs=[smem] + [vmem] * (4 + devices),
        out_specs=[vmem] * half,
        scratch_shapes=[
            pltpu.VMEM((segs, q_heads * HEAD_SIZE), BF),
            pltpu.VMEM((q_heads, segs, 2 * HEAD_SIZE), BF),
            pltpu.VMEM((segs, LANES), F32),
            pltpu.VMEM((LANES, segs), F32),
            pltpu.VMEM((stats, max(strips * width, -(-slots // LANES) * LANES)), F32),
        ],
        compiler_params=params,
        name="attend",
    )(
        me, owner_row, segment_length.reshape(1, segs),
        segment_key_cache.reshape(segs * seg_width, -1),
        segment_value_cache.reshape(segs * seg_width, -1),
        *pieces,
    )
    shares = scatter_blocks(table[:far], table[far:], devices)
    part = pl.pallas_call(
        functools.partial(
            combine_kernel, devices=devices, row_dev=row_dev, width=width, q_heads=q_heads,
            kv_heads=kv_heads, slots=slots,
        ),
        out_shape=split_shapes(devices, (row_dev, d_model)),
        in_specs=[smem] + [vmem] * (1 + devices + far),
        out_specs=[vmem] * half,
        scratch_shapes=[pltpu.VMEM((tall, width), F32), pltpu.VMEM((rows, LANES), F32)],
        compiler_params=params,
        name="combine",
    )(me, out_proj, *pieces, *shares)
    projected = sum(p.astype(F32) for p in scatter_blocks(part[:far], part[far:], devices))
    mixed = (hidden_in.astype(F32) + projected).astype(BF).astype(F32)
    normed = (
        mixed
        * lax.rsqrt(jnp.mean(mixed * mixed, axis=1, keepdims=True) + 1e-06)
        * norm_gain.astype(F32)
    ).astype(BF)
    tokens = gather_blocks(normed, devices)
    ff = w_gate.shape[2]
    moe = pl.pallas_call(
        functools.partial(
            expert_kernel, devices=devices, row_dev=row_dev, top=top, ext_at=ext_at
        ),
        out_shape=split_shapes(devices, (row_dev, d_model)),
        in_specs=[smem] + [vmem] * (3 + 2 * devices),
        out_specs=[vmem] * half,
        scratch_shapes=[pltpu.VMEM((rows, d_model), BF), pltpu.VMEM((rows, ff), BF)],
        compiler_params=pltpu.CompilerParams(vmem_limit_bytes=34 * 1024 * 1024),
        name="experts",
    )(me, w_gate, w_up, w_down, *tokens, *pieces)
    summed = sum(p.astype(F32) for p in scatter_blocks(moe[:far], moe[far:], devices))
    return (mixed + summed).astype(BF)


def solution(mesh):
    both = ("groups", "dev")
    placed = (
        P(both, None), P(both, None), P(both, None, None), P(both, None, None),
        P(both, None, None), P(both), P(both), P(both, None), P(both, None),
        P("dev", None), P(), P("dev", None, None), P("dev", None, None), P("dev", None, None),
    )
    return jax.shard_map(
        on_device, mesh=mesh, in_specs=placed, out_specs=P(both, None), check_vma=False
    )
```

```python
import functools

import jax
import jax.numpy as jnp
from jax import lax
from jax.experimental import pallas as pl
from jax.experimental.pallas import tpu as pltpu
from jax.sharding import PartitionSpec as P


HEAD_SIZE = 128
LANES = 128
NEG = -1e30
BF = jnp.bfloat16
F32 = jnp.float32


def xor_masks(devices):
    far = devices // 4
    return [c + 2 * y + 4 * z for c in range(2) for y in range(2) for z in range(far)]


def swap(x, mask, devices):
    return lax.ppermute(x, "dev", [(i, i ^ mask) for i in range(devices)])


def far_order(devices):
    far = devices // 4
    order = [i for i in range(2, far)]
    return order[:1] + [1] + order[1:] if order else [i for i in range(1, far)]


def gather_blocks(x, devices, mine=None, visit=None):
    far = devices // 4
    near = [x] + [None] * (far - 1)
    for i in far_order(devices):
        near[i] = swap(x, 4 * i, devices)
    if visit is not None:
        near[1] = visit(near[1])
    side = [swap(b, 2, devices) for b in near]
    near_c = [swap(b, 1, devices) for b in near]
    side_c = [swap(b, 1, devices) for b in side]
    if mine is not None:
        near[0] = mine
    return near + side + near_c + side_c


def scatter_blocks(keep, send, devices):
    pieces = []
    for i in reversed(range(devices // 4)):
        pair = keep[i] + swap(send[i], 1, devices)
        mine = pair[0] + swap(pair[1], 2, devices)
        pieces.append(swap(mine, 4 * i, devices) if i else mine)
    return pieces


def split_shapes(devices, tail):
    return [pltpu.VMEM((2,) + tail, BF)] * (devices // 2)


def split_refs(refs, devices):
    far = devices // 4
    return [(refs[c * far + z], y) for c in range(2) for y in range(2) for z in range(far)]


def in_hbm(x):
    return pltpu.with_memory_space_constraint(x, pltpu.HBM)


def in_vmem(x):
    return pltpu.with_memory_space_constraint(x, pltpu.VMEM)


def lane_pick(vec, lane_iota, index):
    return jnp.sum(jnp.where(lane_iota == index, vec, 0.0), axis=1, keepdims=True)


def payload_kernel(
    me_ref, q_ref, fresh_ref, ids_ref, score_ref, owner_ref, length_ref,
    out_ref, mine_ref, meta_ref, turn_scr,
):
    row_dev, qk = q_ref.shape
    kv = fresh_ref.shape[2]
    top = ids_ref.shape[0]
    turn_scr[...] = jnp.zeros(turn_scr.shape, F32)
    turn_scr[0:top, 0:row_dev] = ids_ref[...].astype(F32)
    turn_scr[top : 2 * top, 0:row_dev] = score_ref[...].astype(F32)
    segs = owner_ref.shape[1]
    owner = owner_ref[...]
    first = jnp.broadcast_to(owner[:, 0:1], (row_dev, LANES))
    last = jnp.broadcast_to(owner[:, segs - 1 : segs], (row_dev, LANES))
    lane = lax.broadcasted_iota(jnp.int32, (row_dev, LANES), 1)
    extra = turn_scr[...].T[0:row_dev, :]
    for k, v in enumerate((first // 16, first % 16, last // 16, last % 16)):
        extra = jnp.where(lane == 2 * top + k, v.astype(F32), extra)
    extra = extra.astype(BF)
    for ref in (out_ref, mine_ref):
        ref[:, :qk] = q_ref[...]
        ref[:, qk : qk + kv] = fresh_ref[:, 0, :]
        ref[:, qk + kv : qk + 2 * kv] = fresh_ref[:, 1, :]
        ref[:, qk + 2 * kv :] = extra
    meta_ref[0:1, :] = owner
    meta_ref[1:2, :] = length_ref[...]


def stage_kernel(x_ref, *refs):
    count = (len(refs) - 2) // 2
    ins, out_ref, outs, sems = refs[:count], refs[count], refs[count + 1 : -1], refs[-1]
    copies = [
        pltpu.make_async_copy(a, b, sems.at[i]) for i, (a, b) in enumerate(zip(ins, outs))
    ]
    for c in copies:
        c.start()
    out_ref[...] = x_ref[...]
    for c in copies:
        c.wait()


def attend_kernel(
    me_ref, meta_ref, k_ref, v_ref, *rest,
    devices, row_dev, width, q_heads, kv_heads, slots, seg_width,
):
    pieces = rest[:devices]
    outs = split_refs(rest[devices : devices + devices // 2], devices)
    own_ref, q_scr, o_scr, m_scr, t_scr, l_scr = rest[devices + devices // 2 :]
    kv_mine = (me_ref[0] * (q_heads // devices)) // (q_heads // kv_heads)
    lo = 0
    for start, size in (
        (me_ref[0] * width, width),
        ((q_heads + kv_mine) * HEAD_SIZE, HEAD_SIZE),
        ((q_heads + kv_heads + kv_mine) * HEAD_SIZE, HEAD_SIZE),
        ((q_heads + 2 * kv_heads) * HEAD_SIZE, LANES),
    ):
        for p, piece in enumerate(pieces):
            cut = piece[:, pl.ds(pl.multiple_of(start, LANES), size)]
            own_ref[p * row_dev : (p + 1) * row_dev, lo : lo + size] = cut
        lo += size
    owner_row = meta_ref[0:1, :]
    length_row = meta_ref[1:2, :]
    me = me_ref[0]
    masks = xor_masks(devices)
    rows = devices * row_dev
    segs = meta_ref.shape[1]
    hp = q_heads // devices
    per_kv = q_heads // kv_heads
    qk = q_heads * HEAD_SIZE
    ext = qk + 2 * kv_heads * HEAD_SIZE
    owner_col = jnp.broadcast_to(owner_row.astype(F32), (LANES, segs)).T.astype(jnp.int32)
    hots = []
    per_lane = LANES // row_dev
    lane = lax.broadcasted_iota(jnp.int32, (1, LANES), 1)
    for c in range(rows // LANES):
        gid = jnp.zeros((1, LANES), jnp.int32)
        for i in range(per_lane):
            base = (me ^ masks[c * per_lane + i]) * row_dev - i * row_dev
            gid = jnp.where(lane // row_dev == i, lane + base, gid)
        hots.append((owner_col == gid).astype(F32).astype(BF))
    hot = jnp.concatenate(hots, axis=1)
    step = 512
    for c in range(qk // step):
        block = jnp.concatenate([p[:, c * step : (c + 1) * step] for p in pieces], axis=0)
        q_scr[:, c * step : (c + 1) * step] = jnp.dot(
            hot, block, preferred_element_type=F32
        ).astype(BF)
    group = 16
    wide = group * seg_width
    r_i = lax.broadcasted_iota(jnp.int32, (group, wide), 0)
    c_i = lax.broadcasted_iota(jnp.int32, (group, wide), 1)
    eye_bias = jnp.where(r_i == c_i // seg_width, 0.0, NEG)
    ones = jnp.ones((wide, HEAD_SIZE), BF)
    of_group = lax.broadcasted_iota(jnp.int32, (segs // group, segs), 1) // group
    g_i = lax.broadcasted_iota(jnp.int32, (segs // group, segs), 0)
    lens = jnp.where(of_group == g_i, length_row, 0).astype(F32).astype(BF)
    e_i = lax.broadcasted_iota(jnp.int32, (segs, wide), 0) % group
    e_j = lax.broadcasted_iota(jnp.int32, (segs, wide), 1) // seg_width
    spread = jnp.where(e_i == e_j, 1.0, 0.0).astype(BF)
    live = jnp.dot(lens, spread, preferred_element_type=F32)
    at = (lax.broadcasted_iota(jnp.int32, (segs // group, wide), 1) % seg_width).astype(F32)
    live_bias = jnp.where(at < live, 0.0, NEG)
    stat_lanes = m_scr.shape[1]
    m_lane = lax.broadcasted_iota(jnp.int32, (group, stat_lanes), 1)
    for g in range(segs // group):
        bias = eye_bias + live_bias[g : g + 1, :]
        m_acc = jnp.zeros((group, stat_lanes), F32)
        for kv in range(kv_heads):
            lo = kv * per_kv
            q_tile = jnp.concatenate(
                [
                    q_scr[g * group : (g + 1) * group, (lo + h) * HEAD_SIZE : (lo + h + 1) * HEAD_SIZE]
                    for h in range(per_kv)
                ],
                axis=0,
            )
            k_tile = k_ref[g * wide : (g + 1) * wide, kv * HEAD_SIZE : (kv + 1) * HEAD_SIZE]
            v_tile = v_ref[g * wide : (g + 1) * wide, kv * HEAD_SIZE : (kv + 1) * HEAD_SIZE]
            s = lax.dot_general(
                q_tile, k_tile, (((1,), (1,)), ((), ())), preferred_element_type=F32
            ) * HEAD_SIZE ** (-0.5)
            s = s.reshape(per_kv, group, wide) + bias[None]
            m = jnp.max(s, axis=2, keepdims=True)
            prob = jnp.exp(s - m).reshape(per_kv * group, wide).astype(BF)
            o = jnp.dot(prob, jnp.concatenate([v_tile, ones], axis=1), preferred_element_type=F32)
            o_scr[lo : lo + per_kv, g * group : (g + 1) * group, :] = o.reshape(
                per_kv, group, 2 * HEAD_SIZE
            ).astype(BF)
            for h in range(per_kv):
                m_acc = jnp.where(m_lane == lo + h, m[h], m_acc)
        m_scr[g * group : (g + 1) * group, :] = m_acc
    t_scr[...] = m_scr[...].T
    ext_sum = jnp.zeros((1, LANES), F32)
    for p in range(devices):
        vec = pieces[p][0:1, ext : ext + LANES].astype(F32)
        ext_sum = ext_sum + jnp.where((me ^ masks[p]) == me - 1, vec, 0.0)
    prev_last = 16.0 * lane_pick(ext_sum, lane, 18) + lane_pick(ext_sum, lane, 19)
    owner = owner_row
    first = jnp.min(owner.astype(F32), axis=1, keepdims=True)
    repeated = jnp.logical_and(first == prev_last, me > 0)
    slot = jnp.where(
        jnp.logical_and(owner.astype(F32) == first, repeated), rows + me, owner
    )
    mask = lax.broadcasted_iota(jnp.int32, (slots, segs), 0) == slot
    stats = devices * 8
    st_lane = lax.broadcasted_iota(jnp.int32, (slots, stats), 1)
    max_acc = jnp.zeros((slots, stats), F32)
    sum_acc = jnp.ones((slots, stats), F32)
    for p in range(devices):
        d = me ^ masks[p]
        out_ref, y = outs[p]
        for hh in range(hp):
            h = d * hp + hh
            m_row = t_scr[pl.ds(h, 1), :]
            mm = jnp.where(mask, m_row, NEG)
            r_max = jnp.maximum(jnp.max(mm, axis=1, keepdims=True), 0.1 * NEG)
            weight = jnp.exp(mm - r_max).astype(BF)
            r = jnp.dot(weight, o_scr[h], preferred_element_type=F32)
            r_sum = jnp.maximum(r[:, HEAD_SIZE:], 1.0)
            out_ref[y, 0:slots, hh * HEAD_SIZE : (hh + 1) * HEAD_SIZE] = (
                r[:, :HEAD_SIZE] / r_sum
            ).astype(BF)
            here = jnp.zeros((slots, stats), jnp.bool_)
            for part in range(3):
                here = jnp.logical_or(here, st_lane == d * 8 + part * hp + hh)
            max_acc = jnp.where(here, r_max, max_acc)
            sum_acc = jnp.where(here, r_sum[:, 0:1], sum_acc)
    owned = jnp.max(jnp.where(mask, 1.0, 0.0), axis=1, keepdims=True)
    lse = jnp.where(owned > 0.0, max_acc + jnp.log(sum_acc), 0.0)
    hi = lse.astype(BF).astype(F32)
    rest1 = lse - hi
    mid = rest1.astype(BF).astype(F32)
    low = rest1 - mid
    part = (st_lane % 8) // hp
    lse = jnp.where(part == 0, hi, jnp.where(part == 1, mid, low))
    pad = -(-slots // width) * width - slots
    pad_t = -(-slots // LANES) * LANES - slots
    if pad_t:
        lse = jnp.concatenate([lse, jnp.zeros((pad_t, stats), F32)], axis=0)
    lse_t = lse.T
    if pad > pad_t:
        lse_t = jnp.concatenate([lse_t, jnp.zeros((stats, pad - pad_t), F32)], axis=1)
    l_scr[...] = lse_t
    tail = outs[0][0].shape[1] - slots
    for p in range(devices):
        at = pl.multiple_of((me ^ masks[p]) * 8, 8)
        out_ref, y = outs[p]
        strips = [
            l_scr[pl.ds(at, 8), b * width : (b + 1) * width]
            for b in range((slots + pad) // width)
        ]
        if len(strips) * 8 < tail:
            strips.append(jnp.zeros((tail - len(strips) * 8, width), F32))
        out_ref[y, slots:, :] = jnp.concatenate(strips, axis=0).astype(BF)


def combine_kernel(
    me_ref, w_ref, own_ref, *rest, devices, row_dev, width, q_heads, slots,
):
    far = devices // 4
    shares = rest[:far]
    outs = split_refs(rest[far : far + devices // 2], devices)
    x_scr, l_scr = rest[far + devices // 2 :]
    me = me_ref[0]
    masks = xor_masks(devices)
    rows = devices * row_dev
    hp = q_heads // devices
    ext = width + 2 * HEAD_SIZE
    total = shares[0][...].astype(F32)
    for s in shares[1:]:
        total = total + s[...].astype(F32)
    x_scr[...] = total
    strips = -(-slots // width)
    lse8 = jnp.concatenate(
        [total[slots + 8 * b : slots + 8 * (b + 1), :] for b in range(strips)], axis=1
    )
    lse_rows = [
        lse8[hh : hh + 1, :] + lse8[hp + hh : hp + hh + 1, :] + lse8[2 * hp + hh : 2 * hp + hh + 1, :]
        for hh in range(hp)
    ]
    head_pos = lax.broadcasted_iota(jnp.int32, (LANES, rows), 0)
    spread = jnp.zeros((LANES, rows), F32)
    for hh in range(hp):
        spread = jnp.where(head_pos == hh, lse_rows[hh][:, :rows], spread)
    l_scr[...] = spread.T
    lane = lax.broadcasted_iota(jnp.int32, (1, LANES), 1)
    first = jnp.full((1, LANES), -1.0, F32)
    before = jnp.full((1, LANES), -2.0, F32)
    for p in range(devices):
        vec = own_ref[p * row_dev : p * row_dev + 1, ext : ext + LANES].astype(F32)
        dev = me ^ masks[p]
        first = jnp.where(
            lane == dev, 16.0 * lane_pick(vec, lane, 16) + lane_pick(vec, lane, 17), first
        )
        before = jnp.where(
            lane == dev + 1, 16.0 * lane_pick(vec, lane, 18) + lane_pick(vec, lane, 19), before
        )
    again = jnp.where(jnp.logical_and(first == before, lane < devices), first, -1.0).astype(jnp.int32)
    row_id = jnp.concatenate(
        [
            lax.broadcasted_iota(jnp.int32, (row_dev, LANES), 0) + (me ^ masks[p]) * row_dev
            for p in range(devices)
        ],
        axis=0,
    )
    share = jnp.concatenate(
        [x_scr[pl.ds((me ^ masks[p]) * row_dev, row_dev), :] for p in range(devices)], axis=0
    )
    lse_col = jnp.concatenate(
        [l_scr[pl.ds((me ^ masks[p]) * row_dev, row_dev), :] for p in range(devices)], axis=0
    )
    q = own_ref[:, :width].astype(F32)
    key = own_ref[:, width : width + HEAD_SIZE].astype(F32)
    val = own_ref[:, width + HEAD_SIZE : ext].astype(F32)
    chosen = row_id == again
    heads = []
    for hh in range(hp):
        cut = slice(hh * HEAD_SIZE, (hh + 1) * HEAD_SIZE)
        own = jnp.sum(q[:, cut] * key, axis=1, keepdims=True) * HEAD_SIZE ** (-0.5)
        lse_p = lse_col[:, hh : hh + 1]
        extra = jnp.where(chosen, lse_rows[hh][:, rows : rows + LANES], NEG)
        top = jnp.maximum(jnp.maximum(lse_p, own), jnp.max(extra, axis=1, keepdims=True))
        w_p = jnp.exp(lse_p - top)
        w_o = jnp.exp(own - top)
        w_e = jnp.exp(extra - top)
        more = jnp.concatenate(
            [x_scr[rows:slots, cut], jnp.zeros((LANES - devices, HEAD_SIZE), F32)], axis=0
        )
        num = w_p * share[:, cut] + w_o * val + jnp.dot(
            w_e, more, precision=lax.Precision.HIGHEST, preferred_element_type=F32
        )
        den = w_p + w_o + jnp.sum(w_e, axis=1, keepdims=True)
        heads.append((num / den).astype(BF))
    attn = heads[0] if hp == 1 else jnp.concatenate(heads, axis=1)
    step = 1024
    for c in range(w_ref.shape[1] // step):
        cut = slice(c * step, (c + 1) * step)
        r = jnp.dot(attn, w_ref[:, cut], preferred_element_type=F32).astype(BF)
        for p in range(devices):
            out_ref, y = outs[p]
            out_ref[y, :, cut] = r[p * row_dev : (p + 1) * row_dev]


def expert_kernel(
    me_ref, gate_ref, up_ref, down_ref, own_ref, *rest, devices, row_dev, top, ext_at
):
    pieces = rest[:devices]
    outs = split_refs(rest[devices : devices + devices // 2], devices)
    x_scr, h_scr = rest[devices + devices // 2 :]
    rows = devices * row_dev
    me = me_ref[0].astype(F32)
    for p in range(devices):
        x_scr[p * row_dev : (p + 1) * row_dev, :] = pieces[p][...]
    ff = gate_ref.shape[2]
    d_model = gate_ref.shape[1]
    tile = 256
    for c in range(ff // tile):
        cut = slice(c * tile, (c + 1) * tile)
        a = jnp.dot(x_scr[...], gate_ref[0, :, cut], preferred_element_type=F32)
        b = jnp.dot(x_scr[...], up_ref[0, :, cut], preferred_element_type=F32)
        h_scr[:, cut] = (a / (1.0 + jnp.exp(-a)) * b).astype(BF)
    e = own_ref[:, ext_at : ext_at + LANES].astype(F32)
    lane = lax.broadcasted_iota(jnp.int32, (rows, LANES), 1)
    score = jnp.where(jnp.logical_and(lane >= top, lane < 2 * top), jnp.exp(e * 0.25), 0.0)
    total = jnp.sum(score, axis=1, keepdims=True)
    weight = jnp.zeros((rows, 1), F32)
    for k in range(top):
        weight = weight + jnp.where(e[:, k : k + 1] == me, score[:, top + k : top + k + 1], 0.0)
    weight = weight / total
    step = 512
    for c in range(d_model // step):
        cut = slice(c * step, (c + 1) * step)
        y = jnp.dot(h_scr[...], down_ref[0, :, cut], preferred_element_type=F32)
        y = (y.astype(BF).astype(F32) * weight).astype(BF)
        for p in range(devices):
            out_ref, side = outs[p]
            out_ref[side, :, cut] = y[p * row_dev : (p + 1) * row_dev]


def on_device(
    hidden_in, queries, fresh_key_value, segment_key_cache, segment_value_cache,
    segment_owner_row, segment_length, expert_ids, gate_score, out_proj, norm_gain,
    w_gate, w_up, w_down,
):
    devices = lax.axis_size("dev")
    me = lax.axis_index("dev").astype(jnp.int32).reshape(1)
    row_dev, d_model = hidden_in.shape
    rows = row_dev * devices
    q_heads = queries.shape[1] // HEAD_SIZE
    kv_heads = fresh_key_value.shape[2] // HEAD_SIZE
    segs, seg_width = segment_key_cache.shape[:2]
    top = expert_ids.shape[1]
    width = out_proj.shape[0]
    slots = rows + devices
    strips = -(-slots // width)
    tall = slots + -(-strips // 2) * 16
    smem = pl.BlockSpec(memory_space=pltpu.SMEM)
    vmem = pl.BlockSpec(memory_space=pltpu.VMEM)
    hbm = pl.BlockSpec(memory_space=pltpu.HBM)

    def budget(mib):
        return pltpu.CompilerParams(vmem_limit_bytes=mib * 2**20 * max(1, devices // 16))

    half = devices // 2
    far = devices // 4
    ext_at = (q_heads + 2 * kv_heads) * HEAD_SIZE
    load = jax.ShapeDtypeStruct((row_dev, ext_at + LANES), BF)
    payload, mine, meta = pl.pallas_call(
        payload_kernel,
        out_shape=[load, pltpu.VMEM(load.shape, BF), pltpu.VMEM((8, segs), jnp.int32)],
        in_specs=[smem] + [vmem] * 6,
        out_specs=[vmem] * 3,
        scratch_shapes=[pltpu.VMEM((LANES, LANES), F32)],
        compiler_params=budget(2),
        name="payload",
    )(
        me,
        *map(
            in_hbm,
            (
                queries, fresh_key_value, expert_ids.T, gate_score.T,
                segment_owner_row.reshape(1, segs), segment_length.reshape(1, segs),
            ),
        )
    )
    staged = []

    def stage(x):
        arrays = [
            segment_key_cache.reshape(segs * seg_width, -1),
            segment_value_cache.reshape(segs * seg_width, -1),
            out_proj,
        ]
        x, *copied = pl.pallas_call(
            stage_kernel,
            out_shape=[pltpu.VMEM(a.shape, a.dtype) for a in [x] + arrays],
            in_specs=[vmem] + [hbm] * len(arrays),
            out_specs=[vmem] * (1 + len(arrays)),
            scratch_shapes=[pltpu.SemaphoreType.DMA((len(arrays),))],
            compiler_params=budget(8),
            name="stage",
        )(x, *map(in_hbm, arrays))
        staged.extend(copied)
        return x

    pieces = gather_blocks(payload, devices, mine, stage)
    stats = devices * 8
    own_at = width + 2 * HEAD_SIZE
    *table, own = pl.pallas_call(
        functools.partial(
            attend_kernel, devices=devices, row_dev=row_dev, width=width, q_heads=q_heads,
            kv_heads=kv_heads, slots=slots, seg_width=seg_width,
        ),
        out_shape=split_shapes(devices, (tall, width)) + [pltpu.VMEM((rows, own_at + LANES), BF)],
        in_specs=[smem] + [vmem] * (3 + devices),
        out_specs=[vmem] * (half + 1),
        scratch_shapes=[
            pltpu.VMEM((segs, q_heads * HEAD_SIZE), BF),
            pltpu.VMEM((q_heads, segs, 2 * HEAD_SIZE), BF),
            pltpu.VMEM((segs, LANES), F32),
            pltpu.VMEM((LANES, segs), F32),
            pltpu.VMEM((stats, max(strips * width, -(-slots // LANES) * LANES)), F32),
        ],
        compiler_params=budget(14),
        name="attend",
    )(
        me, meta,
        in_vmem(staged[0]), in_vmem(staged[1]),
        *map(in_vmem, pieces),
    )
    shares = scatter_blocks(table[:far], table[far:], devices)
    part = pl.pallas_call(
        functools.partial(
            combine_kernel, devices=devices, row_dev=row_dev, width=width, q_heads=q_heads,
            slots=slots,
        ),
        out_shape=split_shapes(devices, (row_dev, d_model)),
        in_specs=[smem] + [vmem] * (2 + far),
        out_specs=[vmem] * half,
        scratch_shapes=[pltpu.VMEM((tall, width), F32), pltpu.VMEM((rows, LANES), F32)],
        compiler_params=budget(8),
        name="combine",
    )(me, in_vmem(staged[2]), own, *map(in_vmem, shares))
    projected = sum(p.astype(F32) for p in scatter_blocks(part[:far], part[far:], devices))
    mixed = (hidden_in.astype(F32) + projected).astype(BF).astype(F32)
    normed = (
        mixed
        * lax.rsqrt(jnp.mean(mixed * mixed, axis=1, keepdims=True) + 1e-06)
        * norm_gain.astype(F32)
    ).astype(BF)
    tokens = gather_blocks(normed, devices)
    ff = w_gate.shape[2]
    moe = pl.pallas_call(
        functools.partial(
            expert_kernel, devices=devices, row_dev=row_dev, top=top, ext_at=own_at
        ),
        out_shape=split_shapes(devices, (row_dev, d_model)),
        in_specs=[smem] + [vmem] * (4 + devices),
        out_specs=[vmem] * half,
        scratch_shapes=[
            pltpu.VMEM((rows, d_model), BF),
            pltpu.VMEM((rows, ff), BF),
        ],
        compiler_params=budget(14),
        name="experts",
    )(me, w_gate, w_up, w_down, own, *map(in_vmem, tokens))
    summed = sum(p.astype(F32) for p in scatter_blocks(moe[:far], moe[far:], devices))
    return (mixed + summed).astype(BF)


def solution(mesh):
    both = ("groups", "dev")
    placed = (
        P(both, None), P(both, None), P(both, None, None), P(both, None, None),
        P(both, None, None), P(both), P(both), P(both, None), P(both, None),
        P("dev", None), P(), P("dev", None, None), P("dev", None, None), P("dev", None, None),
    )

    return jax.shard_map(on_device, mesh=mesh, in_specs=placed, out_specs=P(both, None), check_vma=False)
```

```python
import functools

import jax
import jax.numpy as jnp
from jax import lax
from jax.experimental import pallas as pl
from jax.experimental.pallas import tpu as pltpu
from jax.sharding import PartitionSpec as P


HEAD_SIZE = 128
LANES = 128
NEG = -1e30
BF = jnp.bfloat16
F32 = jnp.float32


def xor_masks(devices):
    far = devices // 4
    return [c + 2 * y + 4 * z for c in range(2) for y in range(2) for z in range(far)]


def swap(x, mask, devices):
    return lax.ppermute(x, "dev", [(i, i ^ mask) for i in range(devices)])


def far_order(devices):
    far = devices // 4
    order = [i for i in range(2, far)]
    return order[:1] + [1] + order[1:] if order else [i for i in range(1, far)]


def gather_blocks(x, devices, mine=None, visit=None):
    far = devices // 4
    near = [x] + [None] * (far - 1)
    for i in far_order(devices):
        near[i] = swap(x, 4 * i, devices)
    if visit is not None:
        near[1] = visit(near[1])
    side = [swap(b, 2, devices) for b in near]
    near_c = [swap(b, 1, devices) for b in near]
    side_c = [swap(b, 1, devices) for b in side]
    if mine is not None:
        near[0] = mine
    return near + side + near_c + side_c


def scatter_blocks(keep, send, devices):
    pieces = []
    for i in reversed(range(devices // 4)):
        pair = keep[i] + swap(send[i], 1, devices)
        mine = pair[0] + swap(pair[1], 2, devices)
        pieces.append(swap(mine, 4 * i, devices) if i else mine)
    return pieces


def scatter_sides(blocks, devices):
    far = devices // 4
    pieces = []
    for i in reversed(range(far)):
        away = blocks[far + i] + swap(blocks[3 * far + i], 1, devices)
        home = blocks[i] + swap(blocks[2 * far + i], 1, devices)
        mine = home + swap(away, 2, devices)
        pieces.append(swap(mine, 4 * i, devices) if i else mine)
    return pieces


def split_shapes(devices, tail):
    return [pltpu.VMEM((2,) + tail, BF)] * (devices // 2)


def split_refs(refs, devices):
    far = devices // 4
    return [(refs[c * far + z], y) for c in range(2) for y in range(2) for z in range(far)]


def in_hbm(x):
    return pltpu.with_memory_space_constraint(x, pltpu.HBM)


def in_vmem(x):
    return pltpu.with_memory_space_constraint(x, pltpu.VMEM)


def lane_pick(vec, lane_iota, index):
    return jnp.sum(jnp.where(lane_iota == index, vec, 0.0), axis=1, keepdims=True)


def payload_kernel(
    me_ref, q_ref, fresh_ref, ids_ref, score_ref, owner_ref, length_ref,
    out_ref, mine_ref, meta_ref, turn_scr,
):
    row_dev, qk = q_ref.shape
    kv = fresh_ref.shape[2]
    top = ids_ref.shape[0]
    turn_scr[...] = jnp.zeros(turn_scr.shape, F32)
    turn_scr[0:top, 0:row_dev] = ids_ref[...].astype(F32)
    turn_scr[top : 2 * top, 0:row_dev] = score_ref[...].astype(F32)
    segs = owner_ref.shape[1]
    owner = owner_ref[...]
    first = jnp.broadcast_to(owner[:, 0:1], (row_dev, LANES))
    last = jnp.broadcast_to(owner[:, segs - 1 : segs], (row_dev, LANES))
    lane = lax.broadcasted_iota(jnp.int32, (row_dev, LANES), 1)
    extra = turn_scr[...].T[0:row_dev, :]
    for k, v in enumerate((first // 16, first % 16, last // 16, last % 16)):
        extra = jnp.where(lane == 2 * top + k, v.astype(F32), extra)
    extra = extra.astype(BF)
    for ref in (out_ref, mine_ref):
        ref[:, :qk] = q_ref[...]
        ref[:, qk : qk + kv] = fresh_ref[:, 0, :]
        ref[:, qk + kv : qk + 2 * kv] = fresh_ref[:, 1, :]
        ref[:, qk + 2 * kv :] = extra
    meta_ref[0:1, :] = owner
    meta_ref[1:2, :] = length_ref[...]


def stage_kernel(x_ref, *refs):
    count = (len(refs) - 2) // 2
    ins, out_ref, outs, sems = refs[:count], refs[count], refs[count + 1 : -1], refs[-1]
    copies = [
        pltpu.make_async_copy(a, b, sems.at[i]) for i, (a, b) in enumerate(zip(ins, outs))
    ]
    for c in copies:
        c.start()
    out_ref[...] = x_ref[...]
    for c in copies:
        c.wait()


def attend_kernel(
    me_ref, meta_ref, k_ref, v_ref, *rest,
    devices, row_dev, width, q_heads, kv_heads, slots, seg_width,
):
    pieces = rest[:devices]
    outs = split_refs(rest[devices : devices + devices // 2], devices)
    own_ref, q_scr, o_scr, m_scr, t_scr, l_scr = rest[devices + devices // 2 :]
    kv_mine = (me_ref[0] * (q_heads // devices)) // (q_heads // kv_heads)
    lo = 0
    for start, size in (
        (me_ref[0] * width, width),
        ((q_heads + kv_mine) * HEAD_SIZE, HEAD_SIZE),
        ((q_heads + kv_heads + kv_mine) * HEAD_SIZE, HEAD_SIZE),
        ((q_heads + 2 * kv_heads) * HEAD_SIZE, LANES),
    ):
        for p, piece in enumerate(pieces):
            cut = piece[:, pl.ds(pl.multiple_of(start, LANES), size)]
            own_ref[p * row_dev : (p + 1) * row_dev, lo : lo + size] = cut
        lo += size
    owner_row = meta_ref[0:1, :]
    length_row = meta_ref[1:2, :]
    me = me_ref[0]
    masks = xor_masks(devices)
    rows = devices * row_dev
    segs = meta_ref.shape[1]
    hp = q_heads // devices
    per_kv = q_heads // kv_heads
    qk = q_heads * HEAD_SIZE
    ext = qk + 2 * kv_heads * HEAD_SIZE
    owner_col = jnp.broadcast_to(owner_row.astype(F32), (LANES, segs)).T.astype(jnp.int32)
    hots = []
    per_lane = LANES // row_dev
    lane = lax.broadcasted_iota(jnp.int32, (1, LANES), 1)
    for c in range(rows // LANES):
        gid = jnp.zeros((1, LANES), jnp.int32)
        for i in range(per_lane):
            base = (me ^ masks[c * per_lane + i]) * row_dev - i * row_dev
            gid = jnp.where(lane // row_dev == i, lane + base, gid)
        hots.append((owner_col == gid).astype(F32).astype(BF))
    hot = jnp.concatenate(hots, axis=1)
    step = 512
    for c in range(qk // step):
        block = jnp.concatenate([p[:, c * step : (c + 1) * step] for p in pieces], axis=0)
        q_scr[:, c * step : (c + 1) * step] = jnp.dot(
            hot, block, preferred_element_type=F32
        ).astype(BF)
    group = 16
    wide = group * seg_width
    r_i = lax.broadcasted_iota(jnp.int32, (group, wide), 0)
    c_i = lax.broadcasted_iota(jnp.int32, (group, wide), 1)
    eye_bias = jnp.where(r_i == c_i // seg_width, 0.0, NEG)
    ones = jnp.ones((wide, HEAD_SIZE), BF)
    of_group = lax.broadcasted_iota(jnp.int32, (segs // group, segs), 1) // group
    g_i = lax.broadcasted_iota(jnp.int32, (segs // group, segs), 0)
    lens = jnp.where(of_group == g_i, length_row, 0).astype(F32).astype(BF)
    e_i = lax.broadcasted_iota(jnp.int32, (segs, wide), 0) % group
    e_j = lax.broadcasted_iota(jnp.int32, (segs, wide), 1) // seg_width
    spread = jnp.where(e_i == e_j, 1.0, 0.0).astype(BF)
    live = jnp.dot(lens, spread, preferred_element_type=F32)
    at = (lax.broadcasted_iota(jnp.int32, (segs // group, wide), 1) % seg_width).astype(F32)
    live_bias = jnp.where(at < live, 0.0, NEG)
    stat_lanes = m_scr.shape[1]
    m_lane = lax.broadcasted_iota(jnp.int32, (group, stat_lanes), 1)
    for g in range(segs // group):
        bias = eye_bias + live_bias[g : g + 1, :]
        m_acc = jnp.zeros((group, stat_lanes), F32)
        for kv in range(kv_heads):
            lo = kv * per_kv
            q_tile = jnp.concatenate(
                [
                    q_scr[g * group : (g + 1) * group, (lo + h) * HEAD_SIZE : (lo + h + 1) * HEAD_SIZE]
                    for h in range(per_kv)
                ],
                axis=0,
            )
            k_tile = k_ref[g * wide : (g + 1) * wide, kv * HEAD_SIZE : (kv + 1) * HEAD_SIZE]
            v_tile = v_ref[g * wide : (g + 1) * wide, kv * HEAD_SIZE : (kv + 1) * HEAD_SIZE]
            s = lax.dot_general(
                q_tile, k_tile, (((1,), (1,)), ((), ())), preferred_element_type=F32
            ) * HEAD_SIZE ** (-0.5)
            s = s.reshape(per_kv, group, wide) + bias[None]
            m = jnp.max(s, axis=2, keepdims=True)
            prob = jnp.exp(s - m).reshape(per_kv * group, wide).astype(BF)
            o = jnp.dot(prob, jnp.concatenate([v_tile, ones], axis=1), preferred_element_type=F32)
            o_scr[lo : lo + per_kv, g * group : (g + 1) * group, :] = o.reshape(
                per_kv, group, 2 * HEAD_SIZE
            ).astype(BF)
            for h in range(per_kv):
                m_acc = jnp.where(m_lane == lo + h, m[h], m_acc)
        m_scr[g * group : (g + 1) * group, :] = m_acc
    t_scr[...] = m_scr[...].T
    ext_sum = jnp.zeros((1, LANES), F32)
    for p in range(devices):
        vec = pieces[p][0:1, ext : ext + LANES].astype(F32)
        ext_sum = ext_sum + jnp.where((me ^ masks[p]) == me - 1, vec, 0.0)
    prev_last = 16.0 * lane_pick(ext_sum, lane, 18) + lane_pick(ext_sum, lane, 19)
    owner = owner_row
    first = jnp.min(owner.astype(F32), axis=1, keepdims=True)
    repeated = jnp.logical_and(first == prev_last, me > 0)
    slot = jnp.where(
        jnp.logical_and(owner.astype(F32) == first, repeated), rows + me, owner
    )
    mask = lax.broadcasted_iota(jnp.int32, (slots, segs), 0) == slot
    stats = devices * 8
    st_lane = lax.broadcasted_iota(jnp.int32, (slots, stats), 1)
    max_acc = jnp.zeros((slots, stats), F32)
    sum_acc = jnp.ones((slots, stats), F32)
    for p in range(devices):
        d = me ^ masks[p]
        out_ref, y = outs[p]
        for hh in range(hp):
            h = d * hp + hh
            m_row = t_scr[pl.ds(h, 1), :]
            mm = jnp.where(mask, m_row, NEG)
            r_max = jnp.maximum(jnp.max(mm, axis=1, keepdims=True), 0.1 * NEG)
            weight = jnp.exp(mm - r_max).astype(BF)
            r = jnp.dot(weight, o_scr[h], preferred_element_type=F32)
            r_sum = jnp.maximum(r[:, HEAD_SIZE:], 1.0)
            out_ref[y, 0:slots, hh * HEAD_SIZE : (hh + 1) * HEAD_SIZE] = (
                r[:, :HEAD_SIZE] / r_sum
            ).astype(BF)
            here = jnp.zeros((slots, stats), jnp.bool_)
            for part in range(3):
                here = jnp.logical_or(here, st_lane == d * 8 + part * hp + hh)
            max_acc = jnp.where(here, r_max, max_acc)
            sum_acc = jnp.where(here, r_sum[:, 0:1], sum_acc)
    owned = jnp.max(jnp.where(mask, 1.0, 0.0), axis=1, keepdims=True)
    lse = jnp.where(owned > 0.0, max_acc + jnp.log(sum_acc), 0.0)
    hi = lse.astype(BF).astype(F32)
    rest1 = lse - hi
    mid = rest1.astype(BF).astype(F32)
    low = rest1 - mid
    part = (st_lane % 8) // hp
    lse = jnp.where(part == 0, hi, jnp.where(part == 1, mid, low))
    pad = -(-slots // width) * width - slots
    pad_t = -(-slots // LANES) * LANES - slots
    if pad_t:
        lse = jnp.concatenate([lse, jnp.zeros((pad_t, stats), F32)], axis=0)
    lse_t = lse.T
    if pad > pad_t:
        lse_t = jnp.concatenate([lse_t, jnp.zeros((stats, pad - pad_t), F32)], axis=1)
    l_scr[...] = lse_t
    tail = outs[0][0].shape[1] - slots
    for p in range(devices):
        at = pl.multiple_of((me ^ masks[p]) * 8, 8)
        out_ref, y = outs[p]
        strips = [
            l_scr[pl.ds(at, 8), b * width : (b + 1) * width]
            for b in range((slots + pad) // width)
        ]
        if len(strips) * 8 < tail:
            strips.append(jnp.zeros((tail - len(strips) * 8, width), F32))
        out_ref[y, slots:, :] = jnp.concatenate(strips, axis=0).astype(BF)


def combine_kernel(
    me_ref, w_ref, own_ref, *rest, devices, row_dev, width, q_heads, slots,
):
    far = devices // 4
    shares = rest[:far]
    outs = split_refs(rest[far : far + devices // 2], devices)
    x_scr, l_scr = rest[far + devices // 2 :]
    me = me_ref[0]
    masks = xor_masks(devices)
    rows = devices * row_dev
    hp = q_heads // devices
    ext = width + 2 * HEAD_SIZE
    total = shares[0][...].astype(F32)
    for s in shares[1:]:
        total = total + s[...].astype(F32)
    x_scr[...] = total
    strips = -(-slots // width)
    lse8 = jnp.concatenate(
        [total[slots + 8 * b : slots + 8 * (b + 1), :] for b in range(strips)], axis=1
    )
    lse_rows = [
        lse8[hh : hh + 1, :] + lse8[hp + hh : hp + hh + 1, :] + lse8[2 * hp + hh : 2 * hp + hh + 1, :]
        for hh in range(hp)
    ]
    head_pos = lax.broadcasted_iota(jnp.int32, (LANES, rows), 0)
    spread = jnp.zeros((LANES, rows), F32)
    for hh in range(hp):
        spread = jnp.where(head_pos == hh, lse_rows[hh][:, :rows], spread)
    l_scr[...] = spread.T
    lane = lax.broadcasted_iota(jnp.int32, (1, LANES), 1)
    first = jnp.full((1, LANES), -1.0, F32)
    before = jnp.full((1, LANES), -2.0, F32)
    for p in range(devices):
        vec = own_ref[p * row_dev : p * row_dev + 1, ext : ext + LANES].astype(F32)
        dev = me ^ masks[p]
        first = jnp.where(
            lane == dev, 16.0 * lane_pick(vec, lane, 16) + lane_pick(vec, lane, 17), first
        )
        before = jnp.where(
            lane == dev + 1, 16.0 * lane_pick(vec, lane, 18) + lane_pick(vec, lane, 19), before
        )
    again = jnp.where(jnp.logical_and(first == before, lane < devices), first, -1.0).astype(jnp.int32)
    row_id = jnp.concatenate(
        [
            lax.broadcasted_iota(jnp.int32, (row_dev, LANES), 0) + (me ^ masks[p]) * row_dev
            for p in range(devices)
        ],
        axis=0,
    )
    share = jnp.concatenate(
        [x_scr[pl.ds((me ^ masks[p]) * row_dev, row_dev), :] for p in range(devices)], axis=0
    )
    lse_col = jnp.concatenate(
        [l_scr[pl.ds((me ^ masks[p]) * row_dev, row_dev), :] for p in range(devices)], axis=0
    )
    q = own_ref[:, :width].astype(F32)
    key = own_ref[:, width : width + HEAD_SIZE].astype(F32)
    val = own_ref[:, width + HEAD_SIZE : ext].astype(F32)
    chosen = row_id == again
    heads = []
    for hh in range(hp):
        cut = slice(hh * HEAD_SIZE, (hh + 1) * HEAD_SIZE)
        own = jnp.sum(q[:, cut] * key, axis=1, keepdims=True) * HEAD_SIZE ** (-0.5)
        lse_p = lse_col[:, hh : hh + 1]
        extra = jnp.where(chosen, lse_rows[hh][:, rows : rows + LANES], NEG)
        top = jnp.maximum(jnp.maximum(lse_p, own), jnp.max(extra, axis=1, keepdims=True))
        w_p = jnp.exp(lse_p - top)
        w_o = jnp.exp(own - top)
        w_e = jnp.exp(extra - top)
        more = jnp.concatenate(
            [x_scr[rows:slots, cut], jnp.zeros((LANES - devices, HEAD_SIZE), F32)], axis=0
        )
        num = w_p * share[:, cut] + w_o * val + jnp.dot(
            w_e, more, precision=lax.Precision.HIGHEST, preferred_element_type=F32
        )
        den = w_p + w_o + jnp.sum(w_e, axis=1, keepdims=True)
        heads.append((num / den).astype(BF))
    attn = heads[0] if hp == 1 else jnp.concatenate(heads, axis=1)
    step = 1024
    for c in range(w_ref.shape[1] // step):
        cut = slice(c * step, (c + 1) * step)
        r = jnp.dot(attn, w_ref[:, cut], preferred_element_type=F32).astype(BF)
        for p in range(devices):
            out_ref, y = outs[p]
            out_ref[y, :, cut] = r[p * row_dev : (p + 1) * row_dev]


def expert_kernel(
    me_ref, gate_ref, up_ref, down_ref, own_ref, *rest, spots, row_dev, top, ext_at
):
    count = len(spots)
    pieces, outs = rest[:count], rest[count : 2 * count]
    x_scr, h_scr = rest[2 * count :]
    rows = count * row_dev
    me = me_ref[0].astype(F32)
    for p in range(count):
        x_scr[p * row_dev : (p + 1) * row_dev, :] = pieces[p][...]
    ff = gate_ref.shape[2]
    d_model = gate_ref.shape[1]
    tile = 256
    for c in range(ff // tile):
        cut = slice(c * tile, (c + 1) * tile)
        a = jnp.dot(x_scr[...], gate_ref[0, :, cut], preferred_element_type=F32)
        b = jnp.dot(x_scr[...], up_ref[0, :, cut], preferred_element_type=F32)
        h_scr[:, cut] = (a / (1.0 + jnp.exp(-a)) * b).astype(BF)
    e = jnp.concatenate(
        [own_ref[p * row_dev : (p + 1) * row_dev, ext_at : ext_at + LANES] for p in spots], axis=0
    ).astype(F32)
    lane = lax.broadcasted_iota(jnp.int32, (rows, LANES), 1)
    score = jnp.where(jnp.logical_and(lane >= top, lane < 2 * top), jnp.exp(e * 0.25), 0.0)
    total = jnp.sum(score, axis=1, keepdims=True)
    weight = jnp.zeros((rows, 1), F32)
    for k in range(top):
        weight = weight + jnp.where(e[:, k : k + 1] == me, score[:, top + k : top + k + 1], 0.0)
    weight = weight / total
    step = 512
    for c in range(d_model // step):
        cut = slice(c * step, (c + 1) * step)
        y = jnp.dot(h_scr[...], down_ref[0, :, cut], preferred_element_type=F32)
        y = (y.astype(BF).astype(F32) * weight).astype(BF)
        for p in range(count):
            outs[p][:, cut] = y[p * row_dev : (p + 1) * row_dev]


def on_device(
    hidden_in, queries, fresh_key_value, segment_key_cache, segment_value_cache,
    segment_owner_row, segment_length, expert_ids, gate_score, out_proj, norm_gain,
    w_gate, w_up, w_down,
):
    devices = lax.axis_size("dev")
    me = lax.axis_index("dev").astype(jnp.int32).reshape(1)
    row_dev, d_model = hidden_in.shape
    rows = row_dev * devices
    q_heads = queries.shape[1] // HEAD_SIZE
    kv_heads = fresh_key_value.shape[2] // HEAD_SIZE
    segs, seg_width = segment_key_cache.shape[:2]
    top = expert_ids.shape[1]
    width = out_proj.shape[0]
    slots = rows + devices
    strips = -(-slots // width)
    tall = slots + -(-strips // 2) * 16
    smem = pl.BlockSpec(memory_space=pltpu.SMEM)
    vmem = pl.BlockSpec(memory_space=pltpu.VMEM)
    hbm = pl.BlockSpec(memory_space=pltpu.HBM)

    def budget(mib):
        return pltpu.CompilerParams(vmem_limit_bytes=mib * 2**20 * max(1, devices // 16))

    half = devices // 2
    far = devices // 4
    ext_at = (q_heads + 2 * kv_heads) * HEAD_SIZE
    load = jax.ShapeDtypeStruct((row_dev, ext_at + LANES), BF)
    payload, mine, meta = pl.pallas_call(
        payload_kernel,
        out_shape=[load, pltpu.VMEM(load.shape, BF), pltpu.VMEM((8, segs), jnp.int32)],
        in_specs=[smem] + [vmem] * 6,
        out_specs=[vmem] * 3,
        scratch_shapes=[pltpu.VMEM((LANES, LANES), F32)],
        compiler_params=budget(2),
        name="payload",
    )(
        me,
        *map(
            in_hbm,
            (
                queries, fresh_key_value, expert_ids.T, gate_score.T,
                segment_owner_row.reshape(1, segs), segment_length.reshape(1, segs),
            ),
        )
    )
    staged = []

    def stage(x):
        arrays = [
            segment_key_cache.reshape(segs * seg_width, -1),
            segment_value_cache.reshape(segs * seg_width, -1),
            out_proj,
        ]
        x, *copied = pl.pallas_call(
            stage_kernel,
            out_shape=[pltpu.VMEM(a.shape, a.dtype) for a in [x] + arrays],
            in_specs=[vmem] + [hbm] * len(arrays),
            out_specs=[vmem] * (1 + len(arrays)),
            scratch_shapes=[pltpu.SemaphoreType.DMA((len(arrays),))],
            compiler_params=budget(8),
            name="stage",
        )(x, *map(in_hbm, arrays))
        staged.extend(copied)
        return x

    pieces = gather_blocks(payload, devices, mine, stage)
    stats = devices * 8
    own_at = width + 2 * HEAD_SIZE
    *table, own = pl.pallas_call(
        functools.partial(
            attend_kernel, devices=devices, row_dev=row_dev, width=width, q_heads=q_heads,
            kv_heads=kv_heads, slots=slots, seg_width=seg_width,
        ),
        out_shape=split_shapes(devices, (tall, width)) + [pltpu.VMEM((rows, own_at + LANES), BF)],
        in_specs=[smem] + [vmem] * (3 + devices),
        out_specs=[vmem] * (half + 1),
        scratch_shapes=[
            pltpu.VMEM((segs, q_heads * HEAD_SIZE), BF),
            pltpu.VMEM((q_heads, segs, 2 * HEAD_SIZE), BF),
            pltpu.VMEM((segs, LANES), F32),
            pltpu.VMEM((LANES, segs), F32),
            pltpu.VMEM((stats, max(strips * width, -(-slots // LANES) * LANES)), F32),
        ],
        compiler_params=budget(14),
        name="attend",
    )(
        me, meta,
        in_vmem(staged[0]), in_vmem(staged[1]),
        *map(in_vmem, pieces),
    )
    shares = scatter_blocks(table[:far], table[far:], devices)
    part = pl.pallas_call(
        functools.partial(
            combine_kernel, devices=devices, row_dev=row_dev, width=width, q_heads=q_heads,
            slots=slots,
        ),
        out_shape=split_shapes(devices, (row_dev, d_model)),
        in_specs=[smem] + [vmem] * (2 + far),
        out_specs=[vmem] * half,
        scratch_shapes=[pltpu.VMEM((tall, width), F32), pltpu.VMEM((rows, LANES), F32)],
        compiler_params=budget(8),
        name="combine",
    )(me, in_vmem(staged[2]), own, *map(in_vmem, shares))
    projected = sum(p.astype(F32) for p in scatter_blocks(part[:far], part[far:], devices))
    mixed = (hidden_in.astype(F32) + projected).astype(BF).astype(F32)
    normed = (
        mixed
        * lax.rsqrt(jnp.mean(mixed * mixed, axis=1, keepdims=True) + 1e-06)
        * norm_gain.astype(F32)
    ).astype(BF)
    tokens = gather_blocks(normed, devices)
    ff = w_gate.shape[2]
    moe = [None] * devices
    for side in range(2):
        spots = [p for p in range(devices) if p // far % 2 == side]
        call = pl.pallas_call(
            functools.partial(
                expert_kernel, spots=spots, row_dev=row_dev, top=top, ext_at=own_at
            ),
            out_shape=[pltpu.VMEM((row_dev, d_model), BF)] * half,
            in_specs=[smem] + [vmem] * (4 + half),
            out_specs=[vmem] * half,
            scratch_shapes=[
                pltpu.VMEM((half * row_dev, d_model), BF),
                pltpu.VMEM((half * row_dev, ff), BF),
            ],
            compiler_params=budget(14),
        )
        done = call(me, w_gate, w_up, w_down, own, *(in_vmem(tokens[p]) for p in spots))
        for p, y in zip(spots, done):
            moe[p] = y
    summed = sum(p.astype(F32) for p in scatter_sides(moe, devices))
    return (mixed + summed).astype(BF)


def solution(mesh):
    both = ("groups", "dev")
    placed = (
        P(both, None), P(both, None), P(both, None, None), P(both, None, None),
        P(both, None, None), P(both), P(both), P(both, None), P(both, None),
        P("dev", None), P(), P("dev", None, None), P("dev", None, None), P("dev", None, None),
    )

    return jax.shard_map(on_device, mesh=mesh, in_specs=placed, out_specs=P(both, None), check_vma=False)
```
